32 devices in a mesh: src: 4 (over y, x), tgt: 8 (over z, core).
Axes of the slice: x: 2, y: 2, z: 4, core: 2. Of those that a mesh axis runs over, the one named last changes fastest.
Arguments:
- source_values: float32 [16, 65536], P(None, ('src', 'tgt')), may hold values from -6 to 6
- source_phase: float32 [65536], P(('src', 'tgt')), may hold values from -3.140625 to 3.140625
- leaf_interp: bfloat16 [64, 64], replicated, may hold values from -0.75 to 0.75
- level_interp: bfloat16 [11, 2, 64, 64], replicated, may hold values from -0.5 to 0.5
- level_phase: float32 [11, 3, 1024, 64], P(None, None, ('src', 'tgt')), may hold values from -3.140625 to 3.140625
- middle_interp: bfloat16 [64, 64], replicated, may hold values from -0.75 to 0.75
- middle_phase: float32 [2, 1024, 64], P(None, ('src', 'tgt')), may hold values from -3.140625 to 3.140625
- final_phase: float32 [1024, 64], P(('src', 'tgt')), may hold values from -3.140625 to 3.140625
- final_interp: bfloat16 [64, 64], replicated, may hold values from -0.75 to 0.75
- target_phase: float32 [65536], P(('src', 'tgt')), may hold values from -3.140625 to 3.140625
Outputs:
- target_values: float32 [2, 16, 65536], P(None, None, ('src', 'tgt'))
The draws below stay inside these ranges and needn't reach their ends.
All inputs are finite; a program needn't handle non-finite values.
Results may differ from the reference program's by a relative error of at most 0.024.
Values may be sent and summed in bfloat16 or wider, within the bound.
A program may use at most 64 MiB of HBM per device.

```python
import jax
import jax.numpy as jnp

RANK = 64
COLS = 128
RHS = 16
LEAF = 64
BLK_MUL = 1
LOCAL_SRC = 3
LOCAL_TGT = 3
LS = 2
LT = 3
NLEV = 11
BLK = 32
SLOTS = 1024
SOURCES = 65536
N_SRC = 4
N_TGT = 8


def block_scale(key, shape, split, low, top_value):
    level = 1.0
    for axis_at, blocks in split:
        heights = jax.random.uniform(jax.random.fold_in(jax.random.fold_in(key, 6), axis_at), (blocks,), jnp.float32, low / len(split), top_value / len(split))
        level = level * jnp.repeat(jnp.exp(heights), shape[axis_at] // blocks).reshape((-1,) + (1,) * (len(shape) - 1 - axis_at))
    return level


def noise(rng, shape, scale, limit, split=(), dtype=jnp.bfloat16):
    factor_of = block_scale(rng, shape, split, -0.22, 0.18) if split else 1.0
    values = jax.random.normal(rng, shape, jnp.float32) * scale * factor_of
    return jnp.minimum(jnp.maximum(values, -limit), limit).astype(dtype)


def setup_inputs(seed: int = 0) -> dict:
    splits = jax.random.split(jax.random.key(seed), 11)
    source_values = noise(splits[0], (RHS, SOURCES), 1.0, 6.0, ((1, 32),), jnp.float32)
    source_phase = jnp.clip(jax.random.uniform(splits[1], (SOURCES,), jnp.float32, -3.140625, 3.140625), -3.140625, 3.140625)
    leaf_interp = noise(splits[2], (LEAF, RANK), LEAF ** -0.5, 0.75)
    level_interp = noise(splits[3], (NLEV, 2, RANK, RANK), (2 * RANK) ** -0.5, 0.5)
    level_phase = jnp.clip(jax.random.uniform(splits[4], (NLEV, 3, SLOTS, RANK), jnp.float32, -3.140625, 3.140625), -3.140625, 3.140625)
    middle_interp = noise(splits[5], (RANK, RANK), RANK ** -0.5, 0.75)
    middle_phase = jnp.clip(jax.random.uniform(splits[6], (2, SLOTS, RANK), jnp.float32, -3.140625, 3.140625), -3.140625, 3.140625)
    final_phase = jnp.clip(jax.random.uniform(splits[7], (SLOTS, RANK), jnp.float32, -3.140625, 3.140625), -3.140625, 3.140625)
    final_interp = noise(splits[8], (RANK, LEAF), RANK ** -0.5, 0.75)
    target_phase = jnp.clip(jax.random.uniform(splits[9], (SOURCES,), jnp.float32, -3.140625, 3.140625), -3.140625, 3.140625)
    return {"source_values": source_values, "source_phase": source_phase, "leaf_interp": leaf_interp, "level_interp": level_interp, "level_phase": level_phase, "middle_interp": middle_interp, "middle_phase": middle_phase, "final_phase": final_phase, "final_interp": final_interp, "target_phase": target_phase}


def rotate(vectors, angles):
    half_width = angles.shape[-1]
    values = vectors.astype(jnp.float32)
    real_part = values[..., :half_width]
    imag_part = values[..., half_width:]
    cosine = jnp.cos(angles)[:, None, :]
    sine_val = jnp.sin(angles)[:, None, :]
    return jnp.concatenate([real_part * cosine - imag_part * sine_val, real_part * sine_val + imag_part * cosine], -1)


def block_pair(matrix):
    zeros_block = jnp.zeros_like(matrix)
    upper_rows = jnp.concatenate([matrix, zeros_block], 1)
    lower_rows = jnp.concatenate([zeros_block, matrix], 1)
    return jnp.concatenate([upper_rows, lower_rows], 0)


def flip_pairs(coeffs, stride):
    shape = coeffs.shape
    return coeffs.reshape((shape[0] // (2 * stride), 2, stride) + shape[1:])[:, ::-1].reshape(shape)


def translate(coeffs, partner, phases, matrices):
    shape = coeffs.shape
    own_rot = rotate(coeffs, phases[0]).astype(jnp.bfloat16).reshape(-1, shape[2])
    other_rot = rotate(partner, phases[1]).astype(jnp.bfloat16).reshape(-1, shape[2])
    summed = jnp.dot(own_rot, block_pair(matrices[0]), preferred_element_type=jnp.float32)
    summed = summed + jnp.dot(other_rot, block_pair(matrices[1]), preferred_element_type=jnp.float32)
    return rotate(summed.reshape(shape), phases[2]).astype(jnp.bfloat16)


def reference(source_values, source_phase, leaf_interp, level_interp, level_phase, middle_interp, middle_phase, final_phase, final_interp, target_phase):
    cos_src = jnp.cos(source_phase)[None, :]
    sin_src = jnp.sin(source_phase)[None, :]
    modulated = jnp.stack([source_values * cos_src, -source_values * sin_src]).astype(jnp.bfloat16)
    leaf_terms = jnp.dot(modulated.reshape(-1, LEAF), leaf_interp, preferred_element_type=jnp.float32)
    leaf_terms = leaf_terms.reshape(2, RHS, SLOTS, RANK).transpose(2, 1, 0, 3)
    coeffs = leaf_terms.reshape(SLOTS, RHS, COLS).astype(jnp.bfloat16)
    level_index = 0
    for step_index in range(LOCAL_SRC):
        partner = flip_pairs(coeffs, 2 ** step_index)
        coeffs = translate(coeffs, partner, level_phase[level_index], level_interp[level_index])
        level_index += 1
    for step_index in range(LS):
        partner = flip_pairs(coeffs, (SLOTS // N_SRC) * 2 ** step_index)
        coeffs = translate(coeffs, partner, level_phase[level_index], level_interp[level_index])
        level_index += 1
    devices = N_SRC * N_TGT
    regrouped = coeffs.reshape(devices, devices, BLK_MUL, RHS, COLS).transpose(1, 0, 2, 3, 4).reshape(SLOTS, RHS, COLS)
    switched = rotate(regrouped, middle_phase[0]).astype(jnp.bfloat16).reshape(-1, COLS)
    middle_sum = jnp.dot(switched, block_pair(middle_interp), preferred_element_type=jnp.float32)
    coeffs = rotate(middle_sum.reshape(SLOTS, RHS, COLS), middle_phase[1]).astype(jnp.bfloat16)
    for step_index in range(LT):
        partner = flip_pairs(coeffs, BLK * 2 ** step_index)
        coeffs = translate(coeffs, partner, level_phase[level_index], level_interp[level_index])
        level_index += 1
    for step_index in range(LOCAL_TGT):
        partner = flip_pairs(coeffs, 2 ** step_index)
        coeffs = translate(coeffs, partner, level_phase[level_index], level_interp[level_index])
        level_index += 1
    finals = rotate(coeffs, final_phase).astype(jnp.bfloat16)
    finals = finals.reshape(SLOTS, RHS, 2, RANK).transpose(2, 1, 0, 3).reshape(-1, RANK)
    evaluated = jnp.dot(finals, final_interp, preferred_element_type=jnp.float32).reshape(2, RHS, SOURCES)
    cos_tgt = jnp.cos(target_phase)[None, :]
    sin_tgt = jnp.sin(target_phase)[None, :]
    real_out = evaluated[0] * cos_tgt - evaluated[1] * sin_tgt
    imag_out = evaluated[0] * sin_tgt + evaluated[1] * cos_tgt
    return jnp.stack([real_out, imag_out])
```

```python
import functools

import jax
import jax.numpy as jnp
from jax import lax
from jax.experimental import pallas as pl
from jax.experimental.pallas import tpu as pltpu
from jax.sharding import PartitionSpec as P

LOCAL_SRC = 3
LOCAL_TGT = 3
MESH = pl.DeviceIdType.MESH
SRC_GROUPS = (2, 2)
MID_GROUPS = (2, 2)
FIN_GROUPS = (2, 2)
VLIM = 40 * 1024 * 1024
F32 = jnp.float32
BF16 = jnp.bfloat16

PI_HI = 3.140625
PI_LO = 9.67653589793e-4
SIN_C = (2.605166276178326e-06, -0.00019809046357444052, 0.008333050617328575, -0.16666657969904702, 0.9999999957158396)
COS_C = (-2.605107617861078e-07, 2.4760135505794177e-05, -0.0013888360842290288, 0.04166663620890442, -0.49999999356955516, 0.9999999997799034)


def cos_sin(x):
    k = lax.round(x * (1.0 / 3.141592653589793), lax.RoundingMethod.TO_NEAREST_EVEN)
    r = (x - k * PI_HI) - k * PI_LO
    z = r * r
    c = jnp.full_like(z, COS_C[0])
    for a in COS_C[1:]:
        c = c * z + a
    s = jnp.full_like(z, SIN_C[0])
    for a in SIN_C[1:]:
        s = s * z + a
    s = s * r
    half = k * 0.5
    odd = jnp.abs(half - lax.round(half, lax.RoundingMethod.TO_NEAREST_EVEN))
    sign = 1.0 - 4.0 * odd
    return c * sign, s * sign


def lane_low(shape, half):
    return lax.broadcasted_iota(jnp.int32, shape, len(shape) - 1) < half


def dup(x):
    return jnp.concatenate([x, x], -1)


def dup_halves(x, half):
    y = pltpu.roll(x, half, x.ndim - 1)
    low = lane_low(x.shape, half)
    return jnp.where(low, x, y), jnp.where(low, y, x)


def xor_rows(x, h):
    rows = x.shape[0]
    up = pltpu.roll(x, rows - h, 0)
    down = pltpu.roll(x, h, 0)
    row = lax.broadcasted_iota(jnp.int32, x.shape, 0)
    return jnp.where((row // h) % 2 == 0, up, down)


def xor_lead(x, h):
    return jnp.concatenate([x[i ^ h : (i ^ h) + 1] for i in range(x.shape[0])], 0)


def xor_index(i, j, size):
    bit = 1
    res = i
    while bit < size:
        if j & bit:
            res = res + bit * (1 - 2 * lax.rem(i // bit, 2))
        bit *= 2
    return res


def groups_of(n, sizes):
    at, res = 0, []
    for k in sizes:
        if at < n:
            res.append(tuple(range(at, min(at + k, n))))
            at += k
    while at < n:
        res.append(tuple(range(at, min(at + sizes[-1], n))))
        at += sizes[-1]
    return res


def kernel(
    S, T, levels, src_bits, tgt_bits,
    values_h, sphase_h, leaf_h, lint_h, lphase_h, mint_h, mphase_h, fphase_h, fint_h, tphase_h,
    out,
    values, sphase, leaf, lint, lphase, mint, mphase, fphase, fint, tphase, in_sem,
    w, wl, wm, wf, tc, ts, ps_out, ph_src, pk2, pk, ph_tgt, send1, xa, xb, send2, recv2,
    ps_send, ps_recv, pt_send, pt_recv, c1_send, c1_recv, c2_send, c2_recv,
):
    s_me = lax.axis_index("src")
    t_me = lax.axis_index("tgt")
    half = leaf.shape[1]
    wd = 2 * half
    span = T * half
    R = S * T
    rhs = values.shape[0]
    rows = T * rhs
    K = LOCAL_SRC + src_bits
    M = K + tgt_bits
    N = levels

    barrier = pltpu.get_barrier_semaphore()
    for j in range(1, T):
        pl.semaphore_signal(barrier, inc=1, device_id=(s_me, lax.rem(t_me + j, T)), device_id_type=MESH)
    for j in range(1, S):
        pl.semaphore_signal(barrier, inc=1, device_id=(lax.rem(s_me + j, S), t_me), device_id_type=MESH)

    near = LOCAL_SRC + 1
    loads = [
        pltpu.make_async_copy(a, b, in_sem.at[i])
        for i, (a, b) in enumerate(
            (
                (sphase_h, sphase), (lphase_h.at[0:near], lphase.at[0:near]), (leaf_h, leaf),
                (lint_h.at[0:LOCAL_SRC], lint.at[0:LOCAL_SRC]), (values_h, values),
                (lphase_h.at[near:N], lphase.at[near:N]), (mphase_h, mphase),
                (lint_h.at[LOCAL_SRC:N], lint.at[LOCAL_SRC:N]),
                (fphase_h, fphase), (tphase_h, tphase), (mint_h, mint), (fint_h, fint),
            )
        )
    ]
    for load in loads:
        load.start()

    sgn = jnp.where(lane_low((R, wd), half), -1.0, 1.0)

    def put(idx, angle):
        c, s = cos_sin(angle * sgn)
        tc[idx] = c
        ts[idx] = s

    def put_level(n, prev, own, other, h):
        oth = xor_rows(other, h)
        put(2 * n, own if prev is None else prev + own)
        put(2 * n + 1, oth if prev is None else prev + oth)

    def lp(n, q):
        return dup(lphase[n, q])

    I_SEND1, I_MID, I_FIN, I_TGT, I_SRC = (2 * N + i for i in range(5))

    def point_rows(ref):
        lo, hi = dup_halves(ref[...], half)
        n = lo.shape[0]
        return jnp.concatenate([jnp.concatenate([lo[i : i + 1], hi[i : i + 1]], 0) for i in range(n)], 0)

    def fill(dst, r, L):
        z = jnp.zeros_like(L)
        lz = jnp.concatenate([L, z], 1)
        zl = jnp.concatenate([z, L], 1)
        dst[r : r + half, 0:wd] = lz
        dst[r : r + half, wd : 2 * wd] = zl
        dst[r + half : r + wd, 0:wd] = zl
        dst[r + half : r + wd, wd : 2 * wd] = lz

    def blk(i):
        return pl.ds(pl.multiple_of(i * T, T), T)

    def ps_copy(j):
        e = xor_index(s_me, j, S)
        return pltpu.make_async_remote_copy(
            src_ref=ps_out.at[:, blk(e), :], dst_ref=ph_src.at[:, blk(s_me), :],
            send_sem=ps_send, recv_sem=ps_recv, device_id=(e, t_me), device_id_type=MESH,
        )

    def pt_copy(j):
        e = xor_index(t_me, j, T)
        return pltpu.make_async_remote_copy(
            src_ref=pk.at[e], dst_ref=ph_tgt.at[t_me],
            send_sem=pt_send, recv_sem=pt_recv, device_id=(s_me, e), device_id_type=MESH,
        )

    def c1_copy(j):
        e = xor_index(s_me, j, S)
        return pltpu.make_async_remote_copy(
            src_ref=send1.at[j], dst_ref=xa.at[s_me, :, pl.ds(0, wd)],
            send_sem=c1_send, recv_sem=c1_recv, device_id=(e, t_me), device_id_type=MESH,
        )

    def c2_copy(i, j):
        e = xor_index(t_me, j, T)
        return pltpu.make_async_remote_copy(
            src_ref=send2.at[i, e], dst_ref=recv2.at[i, t_me],
            send_sem=c2_send, recv_sem=c2_recv.at[i], device_id=(s_me, e), device_id_type=MESH,
        )

    s_one = (xor_index(s_me, 1, S), t_me)
    t_one = (s_me, xor_index(t_me, 1, T))
    ps_all = pltpu.make_async_remote_copy(
        src_ref=ps_out.at[:, pl.ds(0, R - T), :], dst_ref=ph_src.at[:, pl.ds(0, R - T), :],
        send_sem=ps_send, recv_sem=ps_recv, device_id=s_one, device_id_type=MESH,
    )
    pt_all = pltpu.make_async_remote_copy(
        src_ref=pk.at[pl.ds(0, T - 1)], dst_ref=ph_tgt.at[pl.ds(0, T - 1)],
        send_sem=pt_send, recv_sem=pt_recv, device_id=t_one, device_id_type=MESH,
    )
    c1_all = pltpu.make_async_remote_copy(
        src_ref=send1.at[pl.ds(0, S - 1)], dst_ref=xa.at[pl.ds(0, S - 1), :, pl.ds(0, wd)],
        send_sem=c1_send, recv_sem=c1_recv, device_id=s_one, device_id_type=MESH,
    )

    def c2_all(i, n):
        return pltpu.make_async_remote_copy(
            src_ref=send2.at[pl.ds(i, n), pl.ds(0, T - 1)], dst_ref=recv2.at[pl.ds(i, n), pl.ds(0, T - 1)],
            send_sem=c2_send, recv_sem=c2_recv.at[i], device_id=t_one, device_id_type=MESH,
        )

    def tab(idx, i):
        return tc[idx, blk(i), :][:, None, :], ts[idx, blk(i), :][:, None, :]

    def split(y):
        y = y.reshape(T, rhs, 2 * wd)
        return y[:, :, :wd], y[:, :, wd:]

    def rot(v, sw, idx, i):
        c, s = tab(idx, i)
        return v * c + sw * s

    def dot(x, m):
        return jnp.dot(x, m, preferred_element_type=F32)

    def step(v, sw, n, i, h):
        own = rot(v, sw, 2 * n, i).astype(BF16)
        oth = xor_lead(rot(v, sw, 2 * n + 1, i), h).astype(BF16)
        x = jnp.concatenate([own, oth], -1).reshape(rows, 2 * wd)
        return split(dot(x, w[n]))

    def last_step(v, sw, n, i, h):
        own = rot(v, sw, 2 * n, i).astype(BF16)
        oth = xor_lead(rot(v, sw, 2 * n + 1, i), h).astype(BF16)
        x = jnp.concatenate([own, oth], -1).reshape(rows, 2 * wd)
        return dot(x, w[n, :, :wd]).reshape(T, rhs, wd)

    for load in loads[:4]:
        load.wait()

    c, s = cos_sin(point_rows(sphase))
    tc[I_SRC] = jnp.where(lane_low(c.shape, half), c, -s)
    for n in range(LOCAL_SRC):
        put_level(n, None if n == 0 else lp(n - 1, 2), lp(n, 0), lp(n, 1), 2**n)
    put(I_SEND1, lp(LOCAL_SRC - 1, 2) + lp(LOCAL_SRC, 0))
    fill(wl, 0, leaf[...])
    for n in range(LOCAL_SRC):
        fill(w.at[n], 0, lint[n, 0])
        fill(w.at[n], 2 * half, lint[n, 1])

    def src_part(js):
        blocks = [xor_index(s_me, j, S) for j in js]
        state = []
        for e in blocks:
            at = pl.multiple_of(e * span, span)
            parts = []
            for p in range(T // 2):
                parts.extend(dup_halves(values[:, pl.ds(pl.multiple_of(at + p * wd, wd), wd)], half))
            x = jnp.stack(parts, 0) * tc[I_SRC, blk(e), :][:, None, :]
            state.append(split(dot(x.astype(BF16).reshape(rows, wd), wl[...])))
        for n in range(LOCAL_SRC):
            state = [step(v, sw, n, e, 2**n) for e, (v, sw) in zip(blocks, state)]
        for j, e, (v, sw) in zip(js, blocks, state):
            y = rot(v, sw, I_SEND1, e).astype(BF16).reshape(rows, wd)
            if j:
                send1[j] = y
            else:
                xa[s_me, :, :wd] = y

    def c1_start(js):
        for j in js:
            if j:
                c1_copy(j).start()

    for load in loads[4:7]:
        load.wait()

    def pick(arrays, q):
        a = arrays[2 * q]()
        b = arrays[2 * q + 1]() if 2 * q + 1 < len(arrays) else a
        return jnp.concatenate([a, b], -1)

    src_arrays = [functools.partial(lambda n, q: lphase[n, q], n, q) for n in range(LOCAL_SRC, K) for q in range(3)]
    for q in range(ps_out.shape[0]):
        ps_out[q] = pick(src_arrays, q)

    tgt_arrays = [functools.partial(lambda q: mphase[q], q) for q in range(2)]
    tgt_arrays += [functools.partial(lambda n, q: lphase[n, q], n, q) for n in range(K, M) for q in range(3)]
    tgt_arrays = tgt_arrays[:-1]
    Q = (len(tgt_arrays) + 1) // 2
    for q in range(Q):
        pk2[q * R : (q + 1) * R, :] = pick(tgt_arrays, q)
    for d in range(T):
        pk[d, 0 : Q * S, :] = pk2[pl.ds(d, Q * S, stride=T), :]

    order = [tuple(S - 1 - i for i in g) for g in groups_of(S, SRC_GROUPS)]
    src_part(order[0])
    pl.semaphore_wait(barrier, S - 1 + T - 1)
    for j in range(S - 1, 0, -1):
        ps_copy(j).start()
    c1_start(order[0])
    for j in range(T - 1, 0, -1):
        pt_copy(j).start()
    for js in order[1:]:
        src_part(js)
        c1_start(js)

    for load in loads[7:]:
        load.wait()
    for n in range(LOCAL_SRC, N):
        fill(w.at[n], 0, lint[n, 0])
        fill(w.at[n], 2 * half, lint[n, 1])
    fill(wm, 0, mint[...])
    fill(wf, 0, fint[...])

    ph_src[:, blk(s_me), :] = ps_out[:, blk(s_me), :]
    ph_tgt[t_me] = pk[t_me]

    for n in range(M, N):
        put_level(n, lp(n - 1, 2), lp(n, 0), lp(n, 1), 2 ** (n - M))
    put(I_FIN, lp(N - 1, 2) + dup(fphase[...]))
    put(I_TGT, point_rows(tphase))

    ps_all.wait_recv()
    sang = []
    for q in range(ps_out.shape[0]):
        sang.extend(dup_halves(ph_src[q], half))
    for b in range(src_bits):
        n = LOCAL_SRC + b
        if b == 0:
            put(2 * n + 1, xor_rows(sang[1], T) - sang[0])
        else:
            put_level(n, sang[3 * b - 1], sang[3 * b], sang[3 * b + 1], T * 2**b)

    pt_all.wait_recv()
    ang = []
    for q in range(Q):
        packed = jnp.concatenate([ph_tgt[:, q * S + i, :] for i in range(S)], 0)
        ang.extend(dup_halves(packed, half))
    put(I_MID, sang[3 * src_bits - 1] + ang[0])
    for b in range(tgt_bits):
        n = K + b
        put_level(n, ang[1] if b == 0 else ang[3 * b + 1], ang[3 * b + 2], ang[3 * b + 3], 2**b)

    c1_all.wait_recv()

    bufs = (xa, xb)
    for b in range(src_bits):
        n = LOCAL_SRC + b
        dst = bufs[b % 2]
        for i in range(S):
            if b == 0:
                v = xa[i, :, :wd].astype(F32).reshape(T, rhs, wd)
                sw = pltpu.roll(v, half, 2)
            else:
                v, sw = split(dot(bufs[(b - 1) % 2][i], w[n - 1]))
                dst[i, :, :wd] = rot(v, sw, 2 * n, i).astype(BF16).reshape(rows, wd)
            dst[i ^ 2**b, :, wd:] = rot(v, sw, 2 * n + 1, i).astype(BF16).reshape(rows, wd)

    for blocks in groups_of(S, MID_GROUPS):
        state = [split(dot(bufs[(src_bits - 1) % 2][i], w[K - 1])) for i in blocks]
        state = [rot(v, sw, I_MID, i).astype(BF16).reshape(rows, wd) for i, (v, sw) in zip(blocks, state)]
        state = [split(dot(x, wm[...])) for x in state]
        for b in range(tgt_bits):
            if b < tgt_bits - 1:
                state = [step(v, sw, K + b, i, 2**b) for i, (v, sw) in zip(blocks, state)]
            else:
                state = [last_step(v, sw, K + b, i, 2**b) for i, (v, sw) in zip(blocks, state)]
        for i, v in zip(blocks, state):
            send2[i] = v.astype(BF16)
        for i in blocks:
            for j in range(T - 1, 0, -1):
                c2_copy(i, j).start()
            recv2[i, t_me] = send2[i, t_me]

    low3 = lane_low((rhs, wd), half)

    for blocks in groups_of(S, FIN_GROUPS):
        for i in blocks:
            c2_all(i, 1).wait_recv()
        state = []
        for i in blocks:
            v = recv2[i].astype(F32)
            state.append((v, pltpu.roll(v, half, 2)))
        for n in range(M, N):
            state = [step(v, sw, n, i, 2 ** (n - M)) for i, (v, sw) in zip(blocks, state)]
        state = [rot(v, sw, I_FIN, i).astype(BF16).reshape(rows, wd) for i, (v, sw) in zip(blocks, state)]
        state = [split(dot(x, wf[...])) for x in state]
        for i, (v, sw) in zip(blocks, state):
            r = rot(v, sw, I_TGT, i)
            rr = pltpu.roll(r, half, 2)
            for p in range(T // 2):
                col = pl.ds(i * T * half + p * wd, wd)
                out[0, :, col] = jnp.where(low3, r[2 * p], rr[2 * p + 1])
                out[1, :, col] = jnp.where(low3, rr[2 * p], r[2 * p + 1])
    ps_all.wait_send()
    pt_all.wait_send()
    c1_all.wait_send()
    c2_all(0, S).wait_send()


def shards(
    source_values, source_phase, leaf_interp, level_interp, level_phase,
    middle_interp, middle_phase, final_phase, final_interp, target_phase,
):
    S = lax.axis_size("src")
    T = lax.axis_size("tgt")
    R = level_phase.shape[2]
    assert R == S * T
    rhs = source_values.shape[0]
    half = leaf_interp.shape[1]
    wd = 2 * half
    N = level_phase.shape[0]
    src_bits = S.bit_length() - 1
    tgt_bits = T.bit_length() - 1
    assert N == LOCAL_SRC + src_bits + tgt_bits + LOCAL_TGT
    Q1 = (3 * src_bits + 1) // 2
    Q = (1 + 3 * tgt_bits + 1) // 2
    ntab = 2 * N + 5
    vm = pltpu.VMEM
    dma = pltpu.SemaphoreType.DMA
    args = (
        source_values, source_phase.reshape(-1, wd), leaf_interp, level_interp, level_phase,
        middle_interp, middle_phase, final_phase, final_interp, target_phase.reshape(-1, wd),
    )
    return pl.pallas_call(
        functools.partial(kernel, S, T, N, src_bits, tgt_bits),
        out_shape=pltpu.VMEM((2,) + source_values.shape, F32),
        in_specs=[pl.BlockSpec(memory_space=pltpu.HBM)] * 10,
        out_specs=pl.BlockSpec(memory_space=pltpu.VMEM),
        scratch_shapes=[vm(a.shape, a.dtype) for a in args] + [
            dma((12,)),
            vm((N, 2 * wd, 2 * wd), BF16), vm((wd, 2 * wd), BF16),
            vm((wd, 2 * wd), BF16), vm((wd, 2 * wd), BF16),
            vm((ntab, R, wd), F32), vm((ntab, R, wd), F32),
            vm((Q1, R, wd), F32), vm((Q1, R, wd), F32), vm((Q * R, wd), F32),
            vm((T, Q * S, wd), F32), vm((T, Q * S, wd), F32),
            vm((S, T * rhs, wd), BF16),
            vm((S, T * rhs, 2 * wd), BF16), vm((S, T * rhs, 2 * wd), BF16),
            vm((S, T, rhs, wd), BF16), vm((S, T, rhs, wd), BF16),
            dma(()), dma(()), dma(()), dma(()),
            dma(()), dma(()), dma(()), dma((S,)),
        ],
        compiler_params=pltpu.CompilerParams(
            collective_id=0, has_side_effects=True, vmem_limit_bytes=VLIM
        ),
    )(*[pltpu.with_memory_space_constraint(a, pltpu.HBM) for a in args])


def solution(mesh):
    return jax.shard_map(
        shards,
        mesh=mesh,
        in_specs=(
            P(None, ("src", "tgt")),
            P(("src", "tgt")),
            P(),
            P(),
            P(None, None, ("src", "tgt"), None),
            P(),
            P(None, ("src", "tgt"), None),
            P(("src", "tgt"), None),
            P(),
            P(("src", "tgt")),
        ),
        out_specs=P(None, None, ("src", "tgt")),
        check_vma=False,
    )
```

```python
import functools

import jax
import jax.numpy as jnp
from jax import lax
from jax.experimental import pallas as pl
from jax.experimental.pallas import tpu as pltpu
from jax.sharding import PartitionSpec as P

LOCAL_SRC = 3
LOCAL_TGT = 3
MESH = pl.DeviceIdType.MESH
SRC_GROUPS = (4,)
MID_GROUPS = (4,)
FIN_GROUPS = (4,)
VLIM = 40 * 1024 * 1024
F32 = jnp.float32
BF16 = jnp.bfloat16
SENT = jnp.float32

PI_HI = 3.140625
PI_LO = 9.67653589793e-4
SIN_C = (2.605166276178326e-06, -0.00019809046357444052, 0.008333050617328575, -0.16666657969904702, 0.9999999957158396)
COS_C = (-2.605107617861078e-07, 2.4760135505794177e-05, -0.0013888360842290288, 0.04166663620890442, -0.49999999356955516, 0.9999999997799034)


def cos_sin(x):
    k = lax.round(x * (1.0 / 3.141592653589793), lax.RoundingMethod.TO_NEAREST_EVEN)
    r = (x - k * PI_HI) - k * PI_LO
    z = r * r
    c = jnp.full_like(z, COS_C[0])
    for a in COS_C[1:]:
        c = c * z + a
    s = jnp.full_like(z, SIN_C[0])
    for a in SIN_C[1:]:
        s = s * z + a
    s = s * r
    half = k * 0.5
    odd = jnp.abs(half - lax.round(half, lax.RoundingMethod.TO_NEAREST_EVEN))
    sign = 1.0 - 4.0 * odd
    return c * sign, s * sign


def lane_low(shape, half):
    return lax.broadcasted_iota(jnp.int32, shape, len(shape) - 1) < half


def dup(x):
    return jnp.concatenate([x, x], -1)


def dup_halves(x, half):
    y = pltpu.roll(x, half, x.ndim - 1)
    low = lane_low(x.shape, half)
    return jnp.where(low, x, y), jnp.where(low, y, x)


def xor_rows(x, h):
    rows = x.shape[0]
    up = pltpu.roll(x, rows - h, 0)
    down = pltpu.roll(x, h, 0)
    row = lax.broadcasted_iota(jnp.int32, x.shape, 0)
    return jnp.where((row // h) % 2 == 0, up, down)


def xor_lead(x, h):
    return jnp.concatenate([x[i ^ h : (i ^ h) + 1] for i in range(x.shape[0])], 0)


def xor_index(i, j, size):
    bit = 1
    res = i
    while bit < size:
        if j & bit:
            res = res + bit * (1 - 2 * lax.rem(i // bit, 2))
        bit *= 2
    return res


def encode(x):
    return x


def decode(x):
    return x


def groups_of(n, sizes):
    at, res = 0, []
    for k in sizes:
        if at < n:
            res.append(tuple(range(at, min(at + k, n))))
            at += k
    while at < n:
        res.append(tuple(range(at, min(at + sizes[-1], n))))
        at += sizes[-1]
    return res


def pairs_of(refs):
    return [(refs[i], refs[min(i + 1, len(refs) - 1)]) for i in range(0, len(refs), 2)]


def kernel(
    S, T, levels, src_bits, tgt_bits,
    values_h, sphase_h, leaf_h, lint_h, lphase_h, mint_h, mphase_h, fphase_h, fint_h, tphase_h,
    out,
    values, sphase, leaf, lint, lphase, mint, mphase, fphase, fint, tphase, in_sem,
    w, wl, wm, wf, tc, ts, ps_out, ph_src, pk2, pk, ph_tgt, pk32, send1, xa, xb, send2, recv2,
    ps_send, ps_recv, pt_send, pt_recv, c1_send, c1_recv, c2_send, c2_recv,
):
    s_me = lax.axis_index("src")
    t_me = lax.axis_index("tgt")
    half = leaf.shape[1]
    wd = 2 * half
    span = T * half
    R = S * T
    rhs = values.shape[0]
    rows = T * rhs
    K = LOCAL_SRC + src_bits
    M = K + tgt_bits
    N = levels

    barrier = pltpu.get_barrier_semaphore()
    for j in range(1, T):
        pl.semaphore_signal(barrier, inc=1, device_id=(s_me, lax.rem(t_me + j, T)), device_id_type=MESH)
    for j in range(1, S):
        pl.semaphore_signal(barrier, inc=1, device_id=(lax.rem(s_me + j, S), t_me), device_id_type=MESH)

    near = LOCAL_SRC + 1
    loads = [
        pltpu.make_async_copy(a, b, in_sem.at[i])
        for i, (a, b) in enumerate(
            (
                (sphase_h, sphase), (leaf_h, leaf), (values_h, values),
                (lphase_h.at[0:near], lphase.at[0:near]), (lint_h.at[0:LOCAL_SRC], lint.at[0:LOCAL_SRC]),
                (lphase_h.at[near:N], lphase.at[near:N]), (mphase_h, mphase),
                (lint_h.at[LOCAL_SRC:N], lint.at[LOCAL_SRC:N]),
                (fphase_h, fphase), (tphase_h, tphase), (mint_h, mint), (fint_h, fint),
            )
        )
    ]
    for load in loads:
        load.start()

    low = lane_low((R, wd), half)

    def put(idx, angle):
        c, s = cos_sin(angle)
        tc[idx] = c
        ts[idx] = jnp.where(low, -s, s)

    def put_two(ia, ib, packed):
        c, s = cos_sin(packed)
        cr = pltpu.roll(c, half, 1)
        sr = pltpu.roll(s, half, 1)
        tc[ia] = jnp.where(low, c, cr)
        tc[ib] = jnp.where(low, cr, c)
        ts[ia] = jnp.where(low, -s, sr)
        ts[ib] = jnp.where(low, -sr, s)

    def put_level(n, prev, pair, h):
        packed = jnp.where(low, pair, xor_rows(pair, h))
        put_two(2 * n, 2 * n + 1, packed if prev is None else prev + packed)

    def both(a, b):
        return jnp.concatenate([a, b], -1)

    def lpair(n):
        return both(lphase[n, 0], lphase[n, 1])

    def lp(n, q):
        return dup(lphase[n, q])

    I_SEND1, I_MID, I_FIN, I_TGT, I_SRC = (2 * N + i for i in range(5))

    def point_rows(ref):
        lo, hi = dup_halves(ref[...], half)
        n = lo.shape[0]
        return jnp.concatenate([jnp.concatenate([lo[i : i + 1], hi[i : i + 1]], 0) for i in range(n)], 0)

    def fill(dst, r, L):
        z = jnp.zeros_like(L)
        lz = jnp.concatenate([L, z], 1)
        zl = jnp.concatenate([z, L], 1)
        dst[r : r + half, 0:wd] = lz
        dst[r : r + half, wd : 2 * wd] = zl
        dst[r + half : r + wd, 0:wd] = zl
        dst[r + half : r + wd, wd : 2 * wd] = lz

    def blk(i):
        return pl.ds(pl.multiple_of(i * T, T), T)

    def ps_copy(j):
        e = xor_index(s_me, j, S)
        return pltpu.make_async_remote_copy(
            src_ref=ps_out.at[e], dst_ref=ph_src.at[s_me],
            send_sem=ps_send, recv_sem=ps_recv, device_id=(e, t_me), device_id_type=MESH,
        )

    def pt_copy(j):
        e = xor_index(t_me, j, T)
        return pltpu.make_async_remote_copy(
            src_ref=pk.at[e], dst_ref=ph_tgt.at[t_me],
            send_sem=pt_send, recv_sem=pt_recv, device_id=(s_me, e), device_id_type=MESH,
        )

    def c1_copy(j):
        e = xor_index(s_me, j, S)
        return pltpu.make_async_remote_copy(
            src_ref=send1.at[j], dst_ref=xa.at[s_me, :, pl.ds(0, wd)],
            send_sem=c1_send, recv_sem=c1_recv, device_id=(e, t_me), device_id_type=MESH,
        )

    def c2_copy(j):
        e = xor_index(t_me, j, T)
        return pltpu.make_async_remote_copy(
            src_ref=send2.at[e], dst_ref=recv2.at[t_me],
            send_sem=c2_send, recv_sem=c2_recv, device_id=(s_me, e), device_id_type=MESH,
        )

    s_one = (xor_index(s_me, 1, S), t_me)
    t_one = (s_me, xor_index(t_me, 1, T))
    ps_all = pltpu.make_async_remote_copy(
        src_ref=ps_out.at[pl.ds(0, S - 1)], dst_ref=ph_src.at[pl.ds(0, S - 1)],
        send_sem=ps_send, recv_sem=ps_recv, device_id=s_one, device_id_type=MESH,
    )
    pt_all = pltpu.make_async_remote_copy(
        src_ref=pk.at[pl.ds(0, T - 1)], dst_ref=ph_tgt.at[pl.ds(0, T - 1)],
        send_sem=pt_send, recv_sem=pt_recv, device_id=t_one, device_id_type=MESH,
    )
    c1_all = pltpu.make_async_remote_copy(
        src_ref=send1.at[pl.ds(0, S - 1)], dst_ref=xa.at[pl.ds(0, S - 1), :, pl.ds(0, wd)],
        send_sem=c1_send, recv_sem=c1_recv, device_id=s_one, device_id_type=MESH,
    )

    c2_all = pltpu.make_async_remote_copy(
        src_ref=send2.at[pl.ds(0, T - 1)], dst_ref=recv2.at[pl.ds(0, T - 1)],
        send_sem=c2_send, recv_sem=c2_recv, device_id=t_one, device_id_type=MESH,
    )

    def spread(table, idx, i):
        return jnp.stack([table[idx, pl.ds(i * T + t, 8, stride=0), :] for t in range(T)], 0)

    def tab(idx, i):
        return spread(tc, idx, i), spread(ts, idx, i)

    def split(y):
        y = y.reshape(T, rhs, 2 * wd)
        return y[:, :, :wd], y[:, :, wd:]

    def rot(v, sw, idx, i):
        c, s = tab(idx, i)
        return jnp.concatenate([v[:, r : r + 8] * c + sw[:, r : r + 8] * s for r in range(0, rhs, 8)], 1)

    def dot(x, m):
        return jnp.dot(x, m, preferred_element_type=F32)

    def step(v, sw, n, i, h):
        own = rot(v, sw, 2 * n, i).astype(BF16)
        oth = xor_lead(rot(v, sw, 2 * n + 1, i), h).astype(BF16)
        x = jnp.concatenate([own, oth], -1).reshape(rows, 2 * wd)
        return split(dot(x, w[n]))

    def last_step(v, sw, n, i, h):
        own = rot(v, sw, 2 * n, i).astype(BF16)
        oth = xor_lead(rot(v, sw, 2 * n + 1, i), h).astype(BF16)
        x = jnp.concatenate([own, oth], -1).reshape(rows, 2 * wd)
        return dot(x, w[n, :, :wd]).reshape(T, rhs, wd)

    for load in loads[:3]:
        load.wait()

    c, s = cos_sin(point_rows(sphase))
    tc[I_SRC] = jnp.where(lane_low(c.shape, half), c, -s)
    fill(wl, 0, leaf[...])
    blocks = [xor_index(s_me, j, S) for j in range(S)]

    def leaf_part(e):
        at = pl.multiple_of(e * span, span)
        parts = []
        for p in range(T // 2):
            parts.extend(dup_halves(values[:, pl.ds(pl.multiple_of(at + p * wd, wd), wd)], half))
        c = spread(tc, I_SRC, e)
        x = jnp.stack(parts, 0)
        x = jnp.concatenate([x[:, r : r + 8] * c for r in range(0, rhs, 8)], 1)
        return x.astype(BF16).reshape(rows, wd)

    for j, e in enumerate(blocks):
        xb[j, :, :wd] = leaf_part(e)

    for load in loads[3:7]:
        load.wait()

    for n in range(LOCAL_SRC):
        put_level(n, None if n == 0 else lp(n - 1, 2), lpair(n), 2**n)
        fill(w.at[n], 0, lint[n, 0])
        fill(w.at[n], 2 * half, lint[n, 1])
    put(I_SEND1, lp(LOCAL_SRC - 1, 2) + lp(LOCAL_SRC, 0))

    src_pairs = [(lphase.at[n, 0], lphase.at[n, 1]) for n in range(LOCAL_SRC, K)]
    src_pairs += pairs_of([lphase.at[n, 2] for n in range(LOCAL_SRC, K)])
    tgt_pairs = [(mphase.at[0], mphase.at[1])]
    tgt_pairs += [(lphase.at[n, 0], lphase.at[n, 1]) for n in range(K, M)]
    tgt_pairs += pairs_of([lphase.at[n, 2] for n in range(K, M - 1)])
    Q = len(tgt_pairs)

    def pack():
        for q, (a, b) in enumerate(src_pairs):
            code = encode(both(a[...], b[...]))
            for e in range(S):
                ps_out[e, q * T : (q + 1) * T, :] = code[e * T : (e + 1) * T].astype(SENT)
        for q, (a, b) in enumerate(tgt_pairs):
            pk2[q * R : (q + 1) * R, :] = both(a[...], b[...])
        for d in range(T):
            pk[d] = encode(pk2[pl.ds(d, Q * S, stride=T), :]).astype(SENT)

    pack()
    for js in groups_of(S, SRC_GROUPS):
        state = [split(dot(xb[j, :, :wd], wl[...])) for j in js]
        for n in range(LOCAL_SRC):
            state = [step(v, sw, n, blocks[j], 2**n) for j, (v, sw) in zip(js, state)]
        for j, (v, sw) in zip(js, state):
            y = rot(v, sw, I_SEND1, blocks[j]).astype(BF16).reshape(rows, wd)
            if j:
                send1[j] = y
            else:
                xa[s_me, :, :wd] = y
    pl.semaphore_wait(barrier, S - 1 + T - 1)
    for j in range(S - 1, 0, -1):
        ps_copy(j).start()
    for j in range(T - 1, 0, -1):
        pt_copy(j).start()
    for j in range(S - 1, 0, -1):
        c1_copy(j).start()

    for load in loads[7:]:
        load.wait()
    for n in range(LOCAL_SRC, N):
        fill(w.at[n], 0, lint[n, 0])
        fill(w.at[n], 2 * half, lint[n, 1])
    fill(wm, 0, mint[...])
    fill(wf, 0, fint[...])

    ph_src[s_me] = ps_out[s_me]
    ph_tgt[t_me] = pk[t_me]

    for n in range(M, N):
        put_level(n, lp(n - 1, 2), lpair(n), 2 ** (n - M))
    put_two(I_FIN, I_TGT, jnp.where(low, lp(N - 1, 2) + dup(fphase[...]), point_rows(tphase)))

    ps_all.wait_recv()
    pt_all.wait_recv()
    c1_all.wait_recv()
    got = [decode(ph_src[i].astype(F32)) for i in range(S)]
    sang = [jnp.concatenate([x[q * T : (q + 1) * T] for x in got], 0) for q in range(len(src_pairs))]
    sres = []
    for q in range(src_bits, len(src_pairs)):
        sres.extend(dup_halves(sang[q], half))
    own, oth = dup_halves(sang[0], half)
    put(2 * LOCAL_SRC + 1, xor_rows(oth, T) - own)
    bufs = (xa, xb)
    for b in range(src_bits):
        n = LOCAL_SRC + b
        dst = bufs[b % 2]
        if b:
            put_level(n, sres[b - 1], sang[b], T * 2**b)
        for i in range(S):
            if b == 0:
                v = xa[i, :, :wd].astype(F32).reshape(T, rhs, wd)
                sw = pltpu.roll(v, half, 2)
            else:
                v, sw = split(dot(bufs[(b - 1) % 2][i], w[n - 1]))
                dst[i, :, :wd] = rot(v, sw, 2 * n, i).astype(BF16).reshape(rows, wd)
            dst[i ^ 2**b, :, wd:] = rot(v, sw, 2 * n + 1, i).astype(BF16).reshape(rows, wd)

    for d in range(T):
        pk32[d] = decode(ph_tgt[d].astype(F32))
    tang = [jnp.concatenate([pk32[:, q * S + i, :] for i in range(S)], 0) for q in range(Q)]
    mid0, mid1 = dup_halves(tang[0], half)
    tres = [mid1]
    for q in range(1 + tgt_bits, Q):
        tres.extend(dup_halves(tang[q], half))
    put(I_MID, sres[src_bits - 1] + mid0)
    for b in range(tgt_bits):
        put_level(K + b, tres[b], tang[1 + b], 2**b)

    for blocks in groups_of(S, MID_GROUPS):
        state = [split(dot(bufs[(src_bits - 1) % 2][i], w[K - 1])) for i in blocks]
        state = [rot(v, sw, I_MID, i).astype(BF16).reshape(rows, wd) for i, (v, sw) in zip(blocks, state)]
        state = [split(dot(x, wm[...])) for x in state]
        for b in range(tgt_bits):
            if b < tgt_bits - 1:
                state = [step(v, sw, K + b, i, 2**b) for i, (v, sw) in zip(blocks, state)]
            else:
                state = [last_step(v, sw, K + b, i, 2**b) for i, (v, sw) in zip(blocks, state)]
        for i, v in zip(blocks, state):
            send2[:, i] = v.astype(BF16)
    for j in range(T - 1, 0, -1):
        c2_copy(j).start()
    recv2[t_me] = send2[t_me]

    low3 = lane_low((rhs, wd), half)

    c2_all.wait_recv()
    for blocks in groups_of(S, FIN_GROUPS):
        state = []
        for i in blocks:
            v = recv2[:, i].astype(F32)
            state.append((v, pltpu.roll(v, half, 2)))
        for n in range(M, N):
            state = [step(v, sw, n, i, 2 ** (n - M)) for i, (v, sw) in zip(blocks, state)]
        state = [rot(v, sw, I_FIN, i).astype(BF16).reshape(rows, wd) for i, (v, sw) in zip(blocks, state)]
        state = [split(dot(x, wf[...])) for x in state]
        for i, (v, sw) in zip(blocks, state):
            r = rot(v, sw, I_TGT, i)
            rr = pltpu.roll(r, half, 2)
            for p in range(T // 2):
                col = pl.ds(i * T * half + p * wd, wd)
                out[0, :, col] = jnp.where(low3, r[2 * p], rr[2 * p + 1])
                out[1, :, col] = jnp.where(low3, rr[2 * p], r[2 * p + 1])
    ps_all.wait_send()
    pt_all.wait_send()
    c1_all.wait_send()
    c2_all.wait_send()


def shards(
    source_values, source_phase, leaf_interp, level_interp, level_phase,
    middle_interp, middle_phase, final_phase, final_interp, target_phase,
):
    S = lax.axis_size("src")
    T = lax.axis_size("tgt")
    R = level_phase.shape[2]
    assert R == S * T
    rhs = source_values.shape[0]
    half = leaf_interp.shape[1]
    wd = 2 * half
    N = level_phase.shape[0]
    src_bits = S.bit_length() - 1
    tgt_bits = T.bit_length() - 1
    assert N == LOCAL_SRC + src_bits + tgt_bits + LOCAL_TGT
    Q1 = src_bits + (src_bits + 1) // 2
    Q = 1 + tgt_bits + tgt_bits // 2
    ntab = 2 * N + 5
    vm = pltpu.VMEM
    dma = pltpu.SemaphoreType.DMA
    args = (
        source_values, source_phase.reshape(-1, wd), leaf_interp, level_interp, level_phase,
        middle_interp, middle_phase, final_phase, final_interp, target_phase.reshape(-1, wd),
    )
    return pl.pallas_call(
        functools.partial(kernel, S, T, N, src_bits, tgt_bits),
        out_shape=pltpu.VMEM((2,) + source_values.shape, F32),
        in_specs=[pl.BlockSpec(memory_space=pltpu.HBM)] * 10,
        out_specs=pl.BlockSpec(memory_space=pltpu.VMEM),
        scratch_shapes=[vm(a.shape, a.dtype) for a in args] + [
            dma((12,)),
            vm((N, 2 * wd, 2 * wd), BF16), vm((wd, 2 * wd), BF16),
            vm((wd, 2 * wd), BF16), vm((wd, 2 * wd), BF16),
            vm((ntab, R, wd), F32), vm((ntab, R, wd), F32),
            vm((S, Q1 * T, wd), SENT), vm((S, Q1 * T, wd), SENT), vm((Q * R, wd), F32),
            vm((T, Q * S, wd), SENT), vm((T, Q * S, wd), SENT), vm((T, Q * S, wd), F32),
            vm((S, T * rhs, wd), BF16),
            vm((S, T * rhs, 2 * wd), BF16), vm((S, T * rhs, 2 * wd), BF16),
            vm((T, S, rhs, wd), BF16), vm((T, S, rhs, wd), BF16),
            dma(()), dma(()), dma(()), dma(()),
            dma(()), dma(()), dma(()), dma(()),
        ],
        compiler_params=pltpu.CompilerParams(
            collective_id=0, has_side_effects=True, vmem_limit_bytes=VLIM
        ),
    )(*[pltpu.with_memory_space_constraint(a, pltpu.HBM) for a in args])


def solution(mesh):
    return jax.shard_map(
        shards,
        mesh=mesh,
        in_specs=(
            P(None, ("src", "tgt")),
            P(("src", "tgt")),
            P(),
            P(),
            P(None, None, ("src", "tgt"), None),
            P(),
            P(None, ("src", "tgt"), None),
            P(("src", "tgt"), None),
            P(),
            P(("src", "tgt")),
        ),
        out_specs=P(None, None, ("src", "tgt")),
        check_vma=False,
    )
```

```python
import functools

import jax
import jax.numpy as jnp
from jax import lax
from jax.experimental import pallas as pl
from jax.experimental.pallas import tpu as pltpu
from jax.sharding import PartitionSpec as P

LOCAL_SRC = 3
LOCAL_TGT = 3
MESH = pl.DeviceIdType.MESH
FIRST = 8
AHEAD = 2
MID_GROUPS = (4,)
FIN_GROUPS = (4,)
VLIM = 40 * 1024 * 1024
F32 = jnp.float32
BF16 = jnp.bfloat16
SENT = jnp.bfloat16
SEG = 64

PI_HI = 3.140625
PI_LO = 9.67653589793e-4
SIN_C = (2.605166276178326e-06, -0.00019809046357444052, 0.008333050617328575, -0.16666657969904702, 0.9999999957158396)
COS_C = (-2.605107617861078e-07, 2.4760135505794177e-05, -0.0013888360842290288, 0.04166663620890442, -0.49999999356955516, 0.9999999997799034)


def cos_sin(x):
    k = lax.round(x * (1.0 / 3.141592653589793), lax.RoundingMethod.TO_NEAREST_EVEN)
    r = (x - k * PI_HI) - k * PI_LO
    z = r * r
    c = jnp.full_like(z, COS_C[0])
    for a in COS_C[1:]:
        c = c * z + a
    s = jnp.full_like(z, SIN_C[0])
    for a in SIN_C[1:]:
        s = s * z + a
    s = s * r
    half = k * 0.5
    odd = jnp.abs(half - lax.round(half, lax.RoundingMethod.TO_NEAREST_EVEN))
    sign = 1.0 - 4.0 * odd
    return c * sign, s * sign


def lane_low(shape, half):
    return lax.broadcasted_iota(jnp.int32, shape, len(shape) - 1) < half


def dup(x):
    return jnp.concatenate([x, x], -1)


def dup_halves(x, half):
    y = pltpu.roll(x, half, x.ndim - 1)
    low = lane_low(x.shape, half)
    return jnp.where(low, x, y), jnp.where(low, y, x)


def xor_rows(x, h):
    rows = x.shape[0]
    up = pltpu.roll(x, rows - h, 0)
    down = pltpu.roll(x, h, 0)
    row = lax.broadcasted_iota(jnp.int32, x.shape, 0)
    return jnp.where((row // h) % 2 == 0, up, down)


def xor_lead(x, h):
    return jnp.concatenate([x[i ^ h : (i ^ h) + 1] for i in range(x.shape[0])], 0)


def xor_index(i, j, size):
    bit = 1
    res = i
    while bit < size:
        if j & bit:
            res = res + bit * (1 - 2 * lax.rem(i // bit, 2))
        bit *= 2
    return res


def encode(x):
    a = jnp.abs(x) * (SEG / 3.141592653589793)
    k = jnp.floor(a)
    v = (1.0 + (a - k)) * jnp.exp2(k - SEG / 2)
    return jnp.where(x < 0, -v, v)


def decode(y):
    u = jnp.abs(y)
    k = jnp.floor(jnp.log2(u))
    r = (k + u * jnp.exp2(-k) + (SEG / 2 - 1)) * (3.141592653589793 / SEG)
    return jnp.where(y < 0, -r, r)


def groups_of(n, sizes):
    at, res = 0, []
    for k in sizes:
        if at < n:
            res.append(tuple(range(at, min(at + k, n))))
            at += k
    while at < n:
        res.append(tuple(range(at, min(at + sizes[-1], n))))
        at += sizes[-1]
    return res


def pairs_of(refs):
    return [(refs[i], refs[min(i + 1, len(refs) - 1)]) for i in range(0, len(refs), 2)]


def kernel(
    S, T, levels, src_bits, tgt_bits,
    values_h, sphase_h, leaf_h, lint_h, lphase_h, mint_h, mphase_h, fphase_h, fint_h, tphase_h,
    out,
    values, lint, lphase, points, mats, phases, in_sem,
    w, wl, wm, wf, tc, ts, ps_out, ph_src, pk2, pk, ph_tgt, pk32, send1, xa, xb, send2, recv2,
    ps_send, ps_recv, pt_send, pt_recv, c1_send, c1_recv, c2_send, c2_recv,
):
    s_me = lax.axis_index("src")
    t_me = lax.axis_index("tgt")
    half = mats.shape[1]
    wd = 2 * half
    span = T * half
    R = S * T
    rhs = values.shape[0]
    rows = T * rhs
    K = LOCAL_SRC + src_bits
    M = K + tgt_bits
    N = levels

    barrier = pltpu.get_barrier_semaphore()
    for j in range(1, T):
        pl.semaphore_signal(barrier, inc=1, device_id=(s_me, lax.rem(t_me + j, T)), device_id_type=MESH)
    for j in range(1, S):
        pl.semaphore_signal(barrier, inc=1, device_id=(lax.rem(s_me + j, S), t_me), device_id_type=MESH)

    loads = [
        pltpu.make_async_copy(a, b, in_sem.at[i])
        for a, b, i in (
            (sphase_h, points.at[0], 0), (tphase_h, points.at[1], 0),
            (leaf_h, mats.at[0], 1), (mint_h, mats.at[1], 1), (fint_h, mats.at[2], 1),
            (values_h.at[:, 0:span], values.at[:, 0:span], 2),
            (lphase_h.at[0:K, :, 0:T], lphase.at[0:K, :, 0:T], 3),
            (lint_h.at[0:LOCAL_SRC], lint.at[0:LOCAL_SRC], 4),
            (values_h.at[:, span : S * span], values.at[:, span : S * span], 5),
            (lphase_h.at[0:K, :, T:R], lphase.at[0:K, :, T:R], 6),
            (lphase_h.at[K:N], lphase.at[K:N], 7),
            (mphase_h, phases.at[0:2], 8), (fphase_h, phases.at[2], 8),
            (lint_h.at[LOCAL_SRC:N], lint.at[LOCAL_SRC:N], 9),
        )
    ]
    both_points = pltpu.make_async_copy(points, points, in_sem.at[0])
    all_mats = pltpu.make_async_copy(mats, mats, in_sem.at[1])
    all_phases = pltpu.make_async_copy(phases, phases, in_sem.at[8])
    for load in loads[:FIRST]:
        load.start()

    low = lane_low((R, wd), half)

    def put(idx, angle, at=0):
        n = angle.shape[0]
        c, s = cos_sin(angle)
        tc[idx, at : at + n] = c
        ts[idx, at : at + n] = jnp.where(low[:n], -s, s)

    def put_two(ia, ib, packed, at=0):
        n = packed.shape[0]
        m = low[:n]
        c, s = cos_sin(packed)
        cr = pltpu.roll(c, half, 1)
        sr = pltpu.roll(s, half, 1)
        tc[ia, at : at + n] = jnp.where(m, c, cr)
        tc[ib, at : at + n] = jnp.where(m, cr, c)
        ts[ia, at : at + n] = jnp.where(m, -s, sr)
        ts[ib, at : at + n] = jnp.where(m, -sr, s)

    def put_level(n, prev, pair, h, at=0):
        packed = jnp.where(low[: pair.shape[0]], pair, xor_rows(pair, h))
        put_two(2 * n, 2 * n + 1, packed if prev is None else prev + packed, at)

    def both(a, b):
        return jnp.concatenate([a, b], -1)

    def lpair(n, a=0, b=R):
        return both(lphase[n, 0, a:b], lphase[n, 1, a:b])

    def lp(n, q, a=0, b=R):
        return dup(lphase[n, q, a:b])

    I_SEND1, I_MID, I_FIN, I_TGT, I_SRC = (2 * N + i for i in range(5))

    def point_rows(ref):
        lo, hi = dup_halves(ref[...], half)
        n = lo.shape[0]
        return jnp.concatenate([jnp.concatenate([lo[i : i + 1], hi[i : i + 1]], 0) for i in range(n)], 0)

    def fill(dst, r, L):
        z = jnp.zeros_like(L)
        lz = jnp.concatenate([L, z], 1)
        zl = jnp.concatenate([z, L], 1)
        dst[r : r + half, 0:wd] = lz
        dst[r : r + half, wd : 2 * wd] = zl
        dst[r + half : r + wd, 0:wd] = zl
        dst[r + half : r + wd, wd : 2 * wd] = lz

    def blk(i):
        return pl.ds(pl.multiple_of(i * T, T), T)

    def ps_copy(e):
        return pltpu.make_async_remote_copy(
            src_ref=ps_out.at[e], dst_ref=ph_src.at[s_me],
            send_sem=ps_send, recv_sem=ps_recv, device_id=(e, t_me), device_id_type=MESH,
        )

    def pt_copy(j):
        e = xor_index(t_me, j, T)
        return pltpu.make_async_remote_copy(
            src_ref=pk.at[e], dst_ref=ph_tgt.at[t_me],
            send_sem=pt_send, recv_sem=pt_recv, device_id=(s_me, e), device_id_type=MESH,
        )

    def c1_copy(e):
        return pltpu.make_async_remote_copy(
            src_ref=send1.at[e], dst_ref=xa.at[s_me, :, pl.ds(0, wd)],
            send_sem=c1_send, recv_sem=c1_recv, device_id=(e, t_me), device_id_type=MESH,
        )

    def c2_copy(k):
        e = k + (t_me <= k).astype(jnp.int32)
        return pltpu.make_async_remote_copy(
            src_ref=send2.at[e], dst_ref=recv2.at[t_me],
            send_sem=c2_send, recv_sem=c2_recv, device_id=(s_me, e), device_id_type=MESH,
        )

    def pt_start():
        for j in range(T - 1, 0, -1):
            pt_copy(j).start()

    s_one = (xor_index(s_me, 1, S), t_me)
    t_one = (s_me, xor_index(t_me, 1, T))
    ps_all = pltpu.make_async_remote_copy(
        src_ref=ps_out.at[pl.ds(0, S - 1)], dst_ref=ph_src.at[pl.ds(0, S - 1)],
        send_sem=ps_send, recv_sem=ps_recv, device_id=s_one, device_id_type=MESH,
    )
    pt_all = pltpu.make_async_remote_copy(
        src_ref=pk.at[pl.ds(0, T - 1)], dst_ref=ph_tgt.at[pl.ds(0, T - 1)],
        send_sem=pt_send, recv_sem=pt_recv, device_id=t_one, device_id_type=MESH,
    )
    c1_all = pltpu.make_async_remote_copy(
        src_ref=send1.at[pl.ds(0, S - 1)], dst_ref=xa.at[pl.ds(0, S - 1), :, pl.ds(0, wd)],
        send_sem=c1_send, recv_sem=c1_recv, device_id=s_one, device_id_type=MESH,
    )

    c2_all = pltpu.make_async_remote_copy(
        src_ref=send2.at[pl.ds(0, T - 1)], dst_ref=recv2.at[pl.ds(0, T - 1)],
        send_sem=c2_send, recv_sem=c2_recv, device_id=t_one, device_id_type=MESH,
    )

    def spread(table, idx, i):
        return jnp.stack([table[idx, pl.ds(i * T + t, 8, stride=0), :] for t in range(T)], 0)

    def tab(idx, i):
        return spread(tc, idx, i), spread(ts, idx, i)

    def split(y):
        y = y.reshape(T, rhs, 2 * wd)
        return y[:, :, :wd], y[:, :, wd:]

    def rot(v, sw, idx, i):
        c, s = tab(idx, i)
        return jnp.concatenate([v[:, r : r + 8] * c + sw[:, r : r + 8] * s for r in range(0, rhs, 8)], 1)

    def dot(x, m):
        return jnp.dot(x, m, preferred_element_type=F32)

    def step(v, sw, n, i, h):
        own = rot(v, sw, 2 * n, i).astype(BF16)
        oth = xor_lead(rot(v, sw, 2 * n + 1, i), h).astype(BF16)
        x = jnp.concatenate([own, oth], -1).reshape(rows, 2 * wd)
        return split(dot(x, w[n]))

    def last_step(v, sw, n, i, h):
        own = rot(v, sw, 2 * n, i).astype(BF16)
        oth = xor_lead(rot(v, sw, 2 * n + 1, i), h).astype(BF16)
        x = jnp.concatenate([own, oth], -1).reshape(rows, 2 * wd)
        return dot(x, w[n, :, :wd]).reshape(T, rhs, wd)

    both_points.wait()
    all_mats.wait()
    loads[5].wait()
    for load in loads[FIRST:]:
        load.start()
    c, s = cos_sin(point_rows(points.at[0]))
    tc[I_SRC] = jnp.where(lane_low(c.shape, half), c, -s)
    fill(wl, 0, mats[0])
    def leaf_part(e):
        parts = []
        for p in range(T // 2):
            parts.extend(dup_halves(values[:, e * span + p * wd : e * span + (p + 1) * wd], half))
        c = spread(tc, I_SRC, e)
        x = jnp.stack(parts, 0)
        x = jnp.concatenate([x[:, r : r + 8] * c for r in range(0, rhs, 8)], 1)
        return x.astype(BF16).reshape(rows, wd)

    xb[0, :, :wd] = leaf_part(0)

    loads[6].wait()
    loads[7].wait()

    src_pairs = [(lphase.at[n, 0], lphase.at[n, 1]) for n in range(LOCAL_SRC, K)]
    src_pairs += pairs_of([lphase.at[n, 2] for n in range(LOCAL_SRC, K)])
    tgt_pairs = [(phases.at[0], phases.at[1])]
    tgt_pairs += [(lphase.at[n, 0], lphase.at[n, 1]) for n in range(K, M)]
    tgt_pairs += pairs_of([lphase.at[n, 2] for n in range(K, M - 1)])
    Q = len(tgt_pairs)

    def src_part(blocks):
        a, b = blocks[0] * T, blocks[-1] * T + T
        state = [split(dot(xb[e, :, :wd], wl[...])) for e in blocks]
        for n in range(LOCAL_SRC):
            put_level(n, None if n == 0 else lp(n - 1, 2, a, b), lpair(n, a, b), 2**n, a)
            if blocks[0] == 0:
                fill(w.at[n], 0, lint[n, 0])
                fill(w.at[n], 2 * half, lint[n, 1])
            state = [step(v, sw, n, e, 2**n) for e, (v, sw) in zip(blocks, state)]
        put(I_SEND1, lp(LOCAL_SRC - 1, 2, a, b) + lp(LOCAL_SRC, 0, a, b), a)
        for e, (v, sw) in zip(blocks, state):
            send1[e] = rot(v, sw, I_SEND1, e).astype(BF16).reshape(rows, wd)

    def pack_src(blocks):
        for q, (a, b) in enumerate(src_pairs):
            for e in blocks:
                at = slice(e * T, (e + 1) * T)
                ps_out[e, q * T : (q + 1) * T, :] = encode(both(a[at], b[at])).astype(SENT)

    def pack_tgt():
        for q, (a, b) in enumerate(tgt_pairs):
            pk2[q * R : (q + 1) * R, :] = both(a[...], b[...])
        for d in range(T):
            pk[d] = encode(pk2[pl.ds(d, Q * S, stride=T), :]).astype(SENT)

    pack_src([0])

    def wait_rest():
        loads[8].wait()
        loads[9].wait()

    def pack_rest():
        loads[10].wait()
        all_phases.wait()
        pack_tgt()

    @pl.when(s_me == 0)
    def _():
        wait_rest()
        pack_rest()

    rest = list(range(1, S))

    def src_rest():
        for e in rest:
            xb[e, :, :wd] = leaf_part(e)
        pack_src(rest)
        src_part(rest)

    late = t_me >= T // 2

    @pl.when(jnp.logical_not(late))
    def _():
        src_part([0])

        @pl.when(s_me != 0)
        def _():
            wait_rest()

        src_rest()

    pl.semaphore_wait(barrier, S - 1 + T - 1)

    @pl.when(s_me != 0)
    def _():
        ps_copy(0).start()

    @pl.when(s_me == 0)
    def _():
        pt_start()

    @pl.when(late)
    def _():
        src_part([0])

    @pl.when(s_me != 0)
    def _():
        c1_copy(0).start()

        @pl.when(late)
        def _():
            wait_rest()

        pack_rest()
        pt_start()

    @pl.when(late)
    def _():
        src_rest()

    def others_start():
        for e in rest:
            @pl.when(s_me != e)
            def _():
                ps_copy(e).start()
                c1_copy(e).start()

    @pl.when(s_me != 0)
    def _():
        others_start()

    xa[s_me, :, :wd] = send1[s_me]

    loads[13].wait()
    for n in range(LOCAL_SRC, M):
        fill(w.at[n], 0, lint[n, 0])
        fill(w.at[n], 2 * half, lint[n, 1])
    fill(wm, 0, mats[1])
    ph_src[s_me] = ps_out[s_me]
    ph_tgt[t_me] = pk[t_me]

    @pl.when(s_me == 0)
    def _():
        others_start()

    ps_all.wait_recv()
    got = [decode(ph_src[i].astype(F32)) for i in range(S)]
    sang = [jnp.concatenate([x[q * T : (q + 1) * T] for x in got], 0) for q in range(len(src_pairs))]
    sres = []
    for q in range(src_bits, len(src_pairs)):
        sres.extend(dup_halves(sang[q], half))
    own, oth = dup_halves(sang[0], half)
    put(2 * LOCAL_SRC + 1, xor_rows(oth, T) - own)
    for b in range(1, src_bits):
        put_level(LOCAL_SRC + b, sres[b - 1], sang[b], T * 2**b)
    pt_all.wait_recv()
    for d in range(T):
        pk32[d] = decode(ph_tgt[d].astype(F32))
    tang = [jnp.concatenate([pk32[:, q * S + i, :] for i in range(S)], 0) for q in range(Q)]
    mid0, mid1 = dup_halves(tang[0], half)
    tres = [mid1]
    for q in range(1 + tgt_bits, Q):
        tres.extend(dup_halves(tang[q], half))
    put(I_MID, sres[src_bits - 1] + mid0)
    for b in range(tgt_bits):
        put_level(K + b, tres[b], tang[1 + b], 2**b)
    c1_all.wait_recv()
    bufs = (xa, xb)
    for b in range(src_bits):
        n = LOCAL_SRC + b
        dst = bufs[b % 2]
        for i in range(S):
            if b == 0:
                v = xa[i, :, :wd].astype(F32).reshape(T, rhs, wd)
                sw = pltpu.roll(v, half, 2)
            else:
                v, sw = split(dot(bufs[(b - 1) % 2][i], w[n - 1]))
                dst[i, :, :wd] = rot(v, sw, 2 * n, i).astype(BF16).reshape(rows, wd)
            dst[i ^ 2**b, :, wd:] = rot(v, sw, 2 * n + 1, i).astype(BF16).reshape(rows, wd)

    for blocks in groups_of(S, MID_GROUPS):
        state = [split(dot(bufs[(src_bits - 1) % 2][i], w[K - 1])) for i in blocks]
        state = [rot(v, sw, I_MID, i).astype(BF16).reshape(rows, wd) for i, (v, sw) in zip(blocks, state)]
        state = [split(dot(x, wm[...])) for x in state]
        for b in range(tgt_bits):
            if b < tgt_bits - 1:
                state = [step(v, sw, K + b, i, 2**b) for i, (v, sw) in zip(blocks, state)]
            else:
                state = [last_step(v, sw, K + b, i, 2**b) for i, (v, sw) in zip(blocks, state)]
        for i, v in zip(blocks, state):
            send2[:, i] = v.astype(BF16)
    for k in range(AHEAD):
        c2_copy(k).start()
    for n in range(M, N):
        fill(w.at[n], 0, lint[n, 0])
        fill(w.at[n], 2 * half, lint[n, 1])
    fill(wf, 0, mats[2])
    for n in range(M, N):
        put_level(n, lp(n - 1, 2), lpair(n), 2 ** (n - M))
    put_two(I_FIN, I_TGT, jnp.where(low, lp(N - 1, 2) + dup(phases[2]), point_rows(points.at[1])))
    for k in range(AHEAD, T - 1):
        c2_copy(k).start()
    recv2[t_me] = send2[t_me]

    low3 = lane_low((rhs, wd), half)

    c2_all.wait_recv()
    for blocks in groups_of(S, FIN_GROUPS):
        state = []
        for i in blocks:
            v = recv2[:, i].astype(F32)
            state.append((v, pltpu.roll(v, half, 2)))
        for n in range(M, N):
            state = [step(v, sw, n, i, 2 ** (n - M)) for i, (v, sw) in zip(blocks, state)]
        state = [rot(v, sw, I_FIN, i).astype(BF16).reshape(rows, wd) for i, (v, sw) in zip(blocks, state)]
        state = [split(dot(x, wf[...])) for x in state]
        for i, (v, sw) in zip(blocks, state):
            r = rot(v, sw, I_TGT, i)
            rr = pltpu.roll(r, half, 2)
            for p in range(T // 2):
                col = pl.ds(i * T * half + p * wd, wd)
                out[0, :, col] = jnp.where(low3, r[2 * p], rr[2 * p + 1])
                out[1, :, col] = jnp.where(low3, rr[2 * p], r[2 * p + 1])
    ps_all.wait_send()
    pt_all.wait_send()
    c1_all.wait_send()
    c2_all.wait_send()


def shards(
    source_values, source_phase, leaf_interp, level_interp, level_phase,
    middle_interp, middle_phase, final_phase, final_interp, target_phase,
):
    S = lax.axis_size("src")
    T = lax.axis_size("tgt")
    R = level_phase.shape[2]
    assert R == S * T
    rhs = source_values.shape[0]
    half = leaf_interp.shape[1]
    wd = 2 * half
    N = level_phase.shape[0]
    src_bits = S.bit_length() - 1
    tgt_bits = T.bit_length() - 1
    assert N == LOCAL_SRC + src_bits + tgt_bits + LOCAL_TGT
    Q1 = src_bits + (src_bits + 1) // 2
    Q = 1 + tgt_bits + tgt_bits // 2
    ntab = 2 * N + 5
    vm = pltpu.VMEM
    dma = pltpu.SemaphoreType.DMA
    args = (
        source_values, source_phase.reshape(-1, wd), leaf_interp, level_interp, level_phase,
        middle_interp, middle_phase, final_phase, final_interp, target_phase.reshape(-1, wd),
    )
    return pl.pallas_call(
        functools.partial(kernel, S, T, N, src_bits, tgt_bits),
        out_shape=pltpu.VMEM((2,) + source_values.shape, F32),
        in_specs=[pl.BlockSpec(memory_space=pltpu.HBM)] * 10,
        out_specs=pl.BlockSpec(memory_space=pltpu.VMEM),
        scratch_shapes=[vm(args[i].shape, args[i].dtype) for i in (0, 3, 4)] + [
            vm((2,) + args[1].shape, F32), vm((3, half, half), BF16), vm((3, R, half), F32), dma((10,)),
            vm((N, 2 * wd, 2 * wd), BF16), vm((wd, 2 * wd), BF16),
            vm((wd, 2 * wd), BF16), vm((wd, 2 * wd), BF16),
            vm((ntab, R, wd), F32), vm((ntab, R, wd), F32),
            vm((S, Q1 * T, wd), SENT), vm((S, Q1 * T, wd), SENT), vm((Q * R, wd), F32),
            vm((T, Q * S, wd), SENT), vm((T, Q * S, wd), SENT), vm((T, Q * S, wd), F32),
            vm((S, T * rhs, wd), BF16),
            vm((S, T * rhs, 2 * wd), BF16), vm((S, T * rhs, 2 * wd), BF16),
            vm((T, S, rhs, wd), BF16), vm((T, S, rhs, wd), BF16),
            dma(()), dma(()), dma(()), dma(()),
            dma(()), dma(()), dma(()), dma(()),
        ],
        compiler_params=pltpu.CompilerParams(
            collective_id=0, has_side_effects=True, vmem_limit_bytes=VLIM
        ),
    )(*[pltpu.with_memory_space_constraint(a, pltpu.HBM) for a in args])


def solution(mesh):
    return jax.shard_map(
        shards,
        mesh=mesh,
        in_specs=(
            P(None, ("src", "tgt")),
            P(("src", "tgt")),
            P(),
            P(),
            P(None, None, ("src", "tgt"), None),
            P(),
            P(None, ("src", "tgt"), None),
            P(("src", "tgt"), None),
            P(),
            P(("src", "tgt")),
        ),
        out_specs=P(None, None, ("src", "tgt")),
        check_vma=False,
    )
```

```python
import functools

import jax
import jax.numpy as jnp
from jax import lax
from jax.experimental import pallas as pl
from jax.experimental.pallas import tpu as pltpu
from jax.sharding import PartitionSpec as P

LOCAL_SRC = 3
LOCAL_TGT = 3
MESH = pl.DeviceIdType.MESH
FIRST = 8
AHEAD = 2
MID_GROUPS = (4,)
FIN_GROUPS = (4,)
VLIM = 40 * 1024 * 1024
F32 = jnp.float32
BF16 = jnp.bfloat16
SENT = jnp.bfloat16
SEG = 64

PI_HI = 3.140625
PI_LO = 9.67653589793e-4
SIN_C = (2.605166276178326e-06, -0.00019809046357444052, 0.008333050617328575, -0.16666657969904702, 0.9999999957158396)
COS_C = (-2.605107617861078e-07, 2.4760135505794177e-05, -0.0013888360842290288, 0.04166663620890442, -0.49999999356955516, 0.9999999997799034)


def cos_sin(x):
    k = lax.round(x * (1.0 / 3.141592653589793), lax.RoundingMethod.TO_NEAREST_EVEN)
    r = (x - k * PI_HI) - k * PI_LO
    z = r * r
    c = jnp.full_like(z, COS_C[0])
    for a in COS_C[1:]:
        c = c * z + a
    s = jnp.full_like(z, SIN_C[0])
    for a in SIN_C[1:]:
        s = s * z + a
    s = s * r
    half = k * 0.5
    odd = jnp.abs(half - lax.round(half, lax.RoundingMethod.TO_NEAREST_EVEN))
    sign = 1.0 - 4.0 * odd
    return c * sign, s * sign


def lane_low(shape, half):
    return lax.broadcasted_iota(jnp.int32, shape, len(shape) - 1) < half


def dup(x):
    return jnp.concatenate([x, x], -1)


def dup_halves(x, half):
    y = pltpu.roll(x, half, x.ndim - 1)
    low = lane_low(x.shape, half)
    return jnp.where(low, x, y), jnp.where(low, y, x)


def xor_rows(x, h):
    rows = x.shape[0]
    up = pltpu.roll(x, rows - h, 0)
    down = pltpu.roll(x, h, 0)
    row = lax.broadcasted_iota(jnp.int32, x.shape, 0)
    return jnp.where((row // h) % 2 == 0, up, down)


def xor_lead(x, h):
    return jnp.concatenate([x[i ^ h : (i ^ h) + 1] for i in range(x.shape[0])], 0)


def xor_index(i, j, size):
    bit = 1
    res = i
    while bit < size:
        if j & bit:
            res = res + bit * (1 - 2 * lax.rem(i // bit, 2))
        bit *= 2
    return res


def encode(x):
    a = jnp.abs(x) * (SEG / 3.141592653589793)
    k = jnp.floor(a)
    v = (1.0 + (a - k)) * jnp.exp2(k - SEG / 2)
    return jnp.where(x < 0, -v, v)


def decode(y):
    u = jnp.abs(y)
    k = jnp.floor(jnp.log2(u))
    r = (k + u * jnp.exp2(-k) + (SEG / 2 - 1)) * (3.141592653589793 / SEG)
    return jnp.where(y < 0, -r, r)


def groups_of(n, sizes):
    at, res = 0, []
    for k in sizes:
        if at < n:
            res.append(tuple(range(at, min(at + k, n))))
            at += k
    while at < n:
        res.append(tuple(range(at, min(at + sizes[-1], n))))
        at += sizes[-1]
    return res


def pairs_of(refs):
    return [(refs[i], refs[min(i + 1, len(refs) - 1)]) for i in range(0, len(refs), 2)]


def kernel(
    S, T, levels, src_bits, tgt_bits,
    values_h, sphase_h, leaf_h, lint_h, lphase_h, mint_h, mphase_h, fphase_h, fint_h, tphase_h,
    out,
    values, lint, lphase, points, mats, phases, in_sem,
    w, wl, wm, wf, tc, ts, ps_out, ph_src, pk2, pk, ph_tgt, pk32, send1, xa, xb, send2, recv2,
    ps_send, ps_recv, pt_send, pt_recv, c1_send, c1_recv, c2_send, c2_recv,
):
    s_me = lax.axis_index("src")
    t_me = lax.axis_index("tgt")
    half = mats.shape[1]
    wd = 2 * half
    span = T * half
    R = S * T
    rhs = values.shape[0]
    rows = T * rhs
    K = LOCAL_SRC + src_bits
    M = K + tgt_bits
    N = levels

    barrier = pltpu.get_barrier_semaphore()
    for j in range(1, T):
        pl.semaphore_signal(barrier, inc=1, device_id=(s_me, lax.rem(t_me + j, T)), device_id_type=MESH)
    for j in range(1, S):
        pl.semaphore_signal(barrier, inc=1, device_id=(lax.rem(s_me + j, S), t_me), device_id_type=MESH)

    loads = [
        pltpu.make_async_copy(a, b, in_sem.at[i])
        for a, b, i in (
            (sphase_h, points.at[0], 0), (tphase_h, points.at[1], 0),
            (lphase_h.at[0:K, :, 0:T], lphase.at[0:K, :, 0:T], 3),
            (values_h.at[:, 0:span], values.at[:, 0:span], 2),
            (leaf_h, mats.at[0], 1),
            (lint_h.at[0:LOCAL_SRC], lint.at[0:LOCAL_SRC], 4),
            (mint_h, mats.at[1], 1), (fint_h, mats.at[2], 1),
            (values_h.at[:, span : S * span], values.at[:, span : S * span], 5),
            (lphase_h.at[0:K, :, T:R], lphase.at[0:K, :, T:R], 6),
            (lphase_h.at[K:N], lphase.at[K:N], 7),
            (mphase_h, phases.at[0:2], 8), (fphase_h, phases.at[2], 8),
            (lint_h.at[LOCAL_SRC:N], lint.at[LOCAL_SRC:N], 9),
        )
    ]
    both_points = pltpu.make_async_copy(points, points, in_sem.at[0])
    all_mats = pltpu.make_async_copy(mats, mats, in_sem.at[1])
    all_phases = pltpu.make_async_copy(phases, phases, in_sem.at[8])
    for load in loads[:FIRST]:
        load.start()

    low = lane_low((R, wd), half)

    def put(idx, angle, at=0):
        n = angle.shape[0]
        c, s = cos_sin(angle)
        tc[idx, at : at + n] = c
        ts[idx, at : at + n] = jnp.where(low[:n], -s, s)

    def put_two(ia, ib, packed, at=0):
        n = packed.shape[0]
        m = low[:n]
        c, s = cos_sin(packed)
        cr = pltpu.roll(c, half, 1)
        sr = pltpu.roll(s, half, 1)
        tc[ia, at : at + n] = jnp.where(m, c, cr)
        tc[ib, at : at + n] = jnp.where(m, cr, c)
        ts[ia, at : at + n] = jnp.where(m, -s, sr)
        ts[ib, at : at + n] = jnp.where(m, -sr, s)

    def put_level(n, prev, pair, h, at=0):
        packed = jnp.where(low[: pair.shape[0]], pair, xor_rows(pair, h))
        put_two(2 * n, 2 * n + 1, packed if prev is None else prev + packed, at)

    def both(a, b):
        return jnp.concatenate([a, b], -1)

    def lpair(n, a=0, b=R):
        return both(lphase[n, 0, a:b], lphase[n, 1, a:b])

    def lp(n, q, a=0, b=R):
        return dup(lphase[n, q, a:b])

    I_SEND1, I_MID, I_FIN, I_TGT, I_SRC = (2 * N + i for i in range(5))

    def point_rows(ref):
        lo, hi = dup_halves(ref[...], half)
        n = lo.shape[0]
        return jnp.concatenate([jnp.concatenate([lo[i : i + 1], hi[i : i + 1]], 0) for i in range(n)], 0)

    def fill(dst, r, L):
        z = jnp.zeros_like(L)
        lz = jnp.concatenate([L, z], 1)
        zl = jnp.concatenate([z, L], 1)
        dst[r : r + half, 0:wd] = lz
        dst[r : r + half, wd : 2 * wd] = zl
        dst[r + half : r + wd, 0:wd] = zl
        dst[r + half : r + wd, wd : 2 * wd] = lz

    def blk(i):
        return pl.ds(pl.multiple_of(i * T, T), T)

    def ps_copy(e):
        return pltpu.make_async_remote_copy(
            src_ref=ps_out.at[e], dst_ref=ph_src.at[s_me],
            send_sem=ps_send, recv_sem=ps_recv, device_id=(e, t_me), device_id_type=MESH,
        )

    def pt_copy(j):
        e = xor_index(t_me, j, T)
        return pltpu.make_async_remote_copy(
            src_ref=pk.at[e], dst_ref=ph_tgt.at[t_me],
            send_sem=pt_send, recv_sem=pt_recv, device_id=(s_me, e), device_id_type=MESH,
        )

    def c1_copy(e):
        return pltpu.make_async_remote_copy(
            src_ref=send1.at[e], dst_ref=xa.at[s_me, :, pl.ds(0, wd)],
            send_sem=c1_send, recv_sem=c1_recv, device_id=(e, t_me), device_id_type=MESH,
        )

    def c2_copy(k):
        e = k + (t_me <= k).astype(jnp.int32)
        return pltpu.make_async_remote_copy(
            src_ref=send2.at[e], dst_ref=recv2.at[t_me],
            send_sem=c2_send, recv_sem=c2_recv, device_id=(s_me, e), device_id_type=MESH,
        )

    def pt_start():
        for j in range(T - 1, 0, -1):
            pt_copy(j).start()

    s_one = (xor_index(s_me, 1, S), t_me)
    t_one = (s_me, xor_index(t_me, 1, T))
    ps_all = pltpu.make_async_remote_copy(
        src_ref=ps_out.at[pl.ds(0, S - 1)], dst_ref=ph_src.at[pl.ds(0, S - 1)],
        send_sem=ps_send, recv_sem=ps_recv, device_id=s_one, device_id_type=MESH,
    )
    pt_all = pltpu.make_async_remote_copy(
        src_ref=pk.at[pl.ds(0, T - 1)], dst_ref=ph_tgt.at[pl.ds(0, T - 1)],
        send_sem=pt_send, recv_sem=pt_recv, device_id=t_one, device_id_type=MESH,
    )
    c1_all = pltpu.make_async_remote_copy(
        src_ref=send1.at[pl.ds(0, S - 1)], dst_ref=xa.at[pl.ds(0, S - 1), :, pl.ds(0, wd)],
        send_sem=c1_send, recv_sem=c1_recv, device_id=s_one, device_id_type=MESH,
    )

    c2_all = pltpu.make_async_remote_copy(
        src_ref=send2.at[pl.ds(0, T - 1)], dst_ref=recv2.at[pl.ds(0, T - 1)],
        send_sem=c2_send, recv_sem=c2_recv, device_id=t_one, device_id_type=MESH,
    )

    def spread(table, idx, i):
        return jnp.stack([table[idx, pl.ds(i * T + t, 8, stride=0), :] for t in range(T)], 0)

    def tab(idx, i):
        return spread(tc, idx, i), spread(ts, idx, i)

    def split(y):
        y = y.reshape(T, rhs, 2 * wd)
        return y[:, :, :wd], y[:, :, wd:]

    def rot(v, sw, idx, i):
        c, s = tab(idx, i)
        return jnp.concatenate([v[:, r : r + 8] * c + sw[:, r : r + 8] * s for r in range(0, rhs, 8)], 1)

    def dot(x, m):
        return jnp.dot(x, m, preferred_element_type=F32)

    def step(v, sw, n, i, h):
        own = rot(v, sw, 2 * n, i).astype(BF16)
        oth = xor_lead(rot(v, sw, 2 * n + 1, i), h).astype(BF16)
        x = jnp.concatenate([own, oth], -1).reshape(rows, 2 * wd)
        return split(dot(x, w[n]))

    def last_step(v, sw, n, i, h):
        own = rot(v, sw, 2 * n, i).astype(BF16)
        oth = xor_lead(rot(v, sw, 2 * n + 1, i), h).astype(BF16)
        x = jnp.concatenate([own, oth], -1).reshape(rows, 2 * wd)
        return dot(x, w[n, :, :wd]).reshape(T, rhs, wd)

    both_points.wait()
    all_mats.wait()
    loads[3].wait()
    for load in loads[FIRST:]:
        load.start()
    c, s = cos_sin(point_rows(points.at[0]))
    tc[I_SRC] = jnp.where(lane_low(c.shape, half), c, -s)
    fill(wl, 0, mats[0])
    def leaf_part(e):
        parts = []
        for p in range(T // 2):
            parts.extend(dup_halves(values[:, e * span + p * wd : e * span + (p + 1) * wd], half))
        c = spread(tc, I_SRC, e)
        x = jnp.stack(parts, 0)
        x = jnp.concatenate([x[:, r : r + 8] * c for r in range(0, rhs, 8)], 1)
        return x.astype(BF16).reshape(rows, wd)

    xb[0, :, :wd] = leaf_part(0)

    loads[2].wait()
    loads[5].wait()

    src_pairs = [(lphase.at[n, 0], lphase.at[n, 1]) for n in range(LOCAL_SRC, K)]
    src_pairs += pairs_of([lphase.at[n, 2] for n in range(LOCAL_SRC, K)])
    tgt_pairs = [(phases.at[0], phases.at[1])]
    tgt_pairs += [(lphase.at[n, 0], lphase.at[n, 1]) for n in range(K, M)]
    tgt_pairs += pairs_of([lphase.at[n, 2] for n in range(K, M - 1)])
    Q = len(tgt_pairs)

    def src_part(blocks):
        a, b = blocks[0] * T, blocks[-1] * T + T
        state = [split(dot(xb[e, :, :wd], wl[...])) for e in blocks]
        for n in range(LOCAL_SRC):
            put_level(n, None if n == 0 else lp(n - 1, 2, a, b), lpair(n, a, b), 2**n, a)
            if blocks[0] == 0:
                fill(w.at[n], 0, lint[n, 0])
                fill(w.at[n], 2 * half, lint[n, 1])
            state = [step(v, sw, n, e, 2**n) for e, (v, sw) in zip(blocks, state)]
        put(I_SEND1, lp(LOCAL_SRC - 1, 2, a, b) + lp(LOCAL_SRC, 0, a, b), a)
        for e, (v, sw) in zip(blocks, state):
            send1[e] = rot(v, sw, I_SEND1, e).astype(BF16).reshape(rows, wd)

    def pack_src(blocks):
        for q, (a, b) in enumerate(src_pairs):
            for e in blocks:
                at = slice(e * T, (e + 1) * T)
                ps_out[e, q * T : (q + 1) * T, :] = encode(both(a[at], b[at])).astype(SENT)

    def pack_tgt():
        for q, (a, b) in enumerate(tgt_pairs):
            pk2[q * R : (q + 1) * R, :] = both(a[...], b[...])
        for d in range(T):
            pk[d] = encode(pk2[pl.ds(d, Q * S, stride=T), :]).astype(SENT)

    pack_src([0])

    def wait_rest():
        loads[8].wait()
        loads[9].wait()

    def pack_rest():
        loads[10].wait()
        all_phases.wait()
        pack_tgt()

    @pl.when(s_me == 0)
    def _():
        wait_rest()
        pack_rest()

    rest = list(range(1, S))

    def src_rest():
        for e in rest:
            xb[e, :, :wd] = leaf_part(e)
        pack_src(rest)
        src_part(rest)

    block_ahead = t_me < T // 2
    all_ahead = t_me < T // 4

    @pl.when(block_ahead)
    def _():
        src_part([0])

    @pl.when(all_ahead & (s_me != 0))
    def _():
        wait_rest()

    @pl.when(all_ahead)
    def _():
        src_rest()

    pl.semaphore_wait(barrier, S - 1 + T - 1)

    @pl.when(s_me != 0)
    def _():
        ps_copy(0).start()

    @pl.when(s_me == 0)
    def _():
        pt_start()

    @pl.when(jnp.logical_not(block_ahead))
    def _():
        src_part([0])

    @pl.when(s_me != 0)
    def _():
        c1_copy(0).start()

        @pl.when(jnp.logical_not(all_ahead))
        def _():
            wait_rest()

        pack_rest()
        pt_start()

    @pl.when(jnp.logical_not(all_ahead))
    def _():
        src_rest()

    def others_start():
        for e in rest:
            @pl.when(s_me != e)
            def _():
                ps_copy(e).start()
                c1_copy(e).start()

    @pl.when(s_me != 0)
    def _():
        others_start()

    xa[s_me, :, :wd] = send1[s_me]

    loads[13].wait()
    for n in range(LOCAL_SRC, M):
        fill(w.at[n], 0, lint[n, 0])
        fill(w.at[n], 2 * half, lint[n, 1])
    fill(wm, 0, mats[1])
    ph_src[s_me] = ps_out[s_me]
    ph_tgt[t_me] = pk[t_me]

    @pl.when(s_me == 0)
    def _():
        others_start()

    ps_all.wait_recv()
    got = [decode(ph_src[i].astype(F32)) for i in range(S)]
    sang = [jnp.concatenate([x[q * T : (q + 1) * T] for x in got], 0) for q in range(len(src_pairs))]
    sres = []
    for q in range(src_bits, len(src_pairs)):
        sres.extend(dup_halves(sang[q], half))
    own, oth = dup_halves(sang[0], half)
    put(2 * LOCAL_SRC + 1, xor_rows(oth, T) - own)
    for b in range(1, src_bits):
        put_level(LOCAL_SRC + b, sres[b - 1], sang[b], T * 2**b)
    pt_all.wait_recv()
    for d in range(T):
        pk32[d] = decode(ph_tgt[d].astype(F32))
    tang = [jnp.concatenate([pk32[:, q * S + i, :] for i in range(S)], 0) for q in range(Q)]
    mid0, mid1 = dup_halves(tang[0], half)
    tres = [mid1]
    for q in range(1 + tgt_bits, Q):
        tres.extend(dup_halves(tang[q], half))
    put(I_MID, sres[src_bits - 1] + mid0)
    for b in range(tgt_bits):
        put_level(K + b, tres[b], tang[1 + b], 2**b)
    c1_all.wait_recv()
    bufs = (xa, xb)
    for b in range(src_bits):
        n = LOCAL_SRC + b
        dst = bufs[b % 2]
        for i in range(S):
            if b == 0:
                v = xa[i, :, :wd].astype(F32).reshape(T, rhs, wd)
                sw = pltpu.roll(v, half, 2)
            else:
                v, sw = split(dot(bufs[(b - 1) % 2][i], w[n - 1]))
                dst[i, :, :wd] = rot(v, sw, 2 * n, i).astype(BF16).reshape(rows, wd)
            dst[i ^ 2**b, :, wd:] = rot(v, sw, 2 * n + 1, i).astype(BF16).reshape(rows, wd)

    for blocks in groups_of(S, MID_GROUPS):
        state = [split(dot(bufs[(src_bits - 1) % 2][i], w[K - 1])) for i in blocks]
        state = [rot(v, sw, I_MID, i).astype(BF16).reshape(rows, wd) for i, (v, sw) in zip(blocks, state)]
        state = [split(dot(x, wm[...])) for x in state]
        for b in range(tgt_bits):
            if b < tgt_bits - 1:
                state = [step(v, sw, K + b, i, 2**b) for i, (v, sw) in zip(blocks, state)]
            else:
                state = [last_step(v, sw, K + b, i, 2**b) for i, (v, sw) in zip(blocks, state)]
        for i, v in zip(blocks, state):
            send2[:, i] = v.astype(BF16)
    for k in range(AHEAD):
        c2_copy(k).start()
    for n in range(M, N):
        fill(w.at[n], 0, lint[n, 0])
        fill(w.at[n], 2 * half, lint[n, 1])
    fill(wf, 0, mats[2])
    for n in range(M, N):
        put_level(n, lp(n - 1, 2), lpair(n), 2 ** (n - M))
    put_two(I_FIN, I_TGT, jnp.where(low, lp(N - 1, 2) + dup(phases[2]), point_rows(points.at[1])))
    for k in range(AHEAD, T - 1):
        c2_copy(k).start()
    recv2[t_me] = send2[t_me]

    low3 = lane_low((rhs, wd), half)

    c2_all.wait_recv()
    for blocks in groups_of(S, FIN_GROUPS):
        state = []
        for i in blocks:
            v = recv2[:, i].astype(F32)
            state.append((v, pltpu.roll(v, half, 2)))
        for n in range(M, N):
            state = [step(v, sw, n, i, 2 ** (n - M)) for i, (v, sw) in zip(blocks, state)]
        state = [rot(v, sw, I_FIN, i).astype(BF16).reshape(rows, wd) for i, (v, sw) in zip(blocks, state)]
        state = [split(dot(x, wf[...])) for x in state]
        for i, (v, sw) in zip(blocks, state):
            r = rot(v, sw, I_TGT, i)
            rr = pltpu.roll(r, half, 2)
            for p in range(T // 2):
                col = pl.ds(i * T * half + p * wd, wd)
                out[0, :, col] = jnp.where(low3, r[2 * p], rr[2 * p + 1])
                out[1, :, col] = jnp.where(low3, rr[2 * p], r[2 * p + 1])
    ps_all.wait_send()
    pt_all.wait_send()
    c1_all.wait_send()
    c2_all.wait_send()


def shards(
    source_values, source_phase, leaf_interp, level_interp, level_phase,
    middle_interp, middle_phase, final_phase, final_interp, target_phase,
):
    S = lax.axis_size("src")
    T = lax.axis_size("tgt")
    R = level_phase.shape[2]
    assert R == S * T
    rhs = source_values.shape[0]
    half = leaf_interp.shape[1]
    wd = 2 * half
    N = level_phase.shape[0]
    src_bits = S.bit_length() - 1
    tgt_bits = T.bit_length() - 1
    assert N == LOCAL_SRC + src_bits + tgt_bits + LOCAL_TGT
    Q1 = src_bits + (src_bits + 1) // 2
    Q = 1 + tgt_bits + tgt_bits // 2
    ntab = 2 * N + 5
    vm = pltpu.VMEM
    dma = pltpu.SemaphoreType.DMA
    args = (
        source_values, source_phase.reshape(-1, wd), leaf_interp, level_interp, level_phase,
        middle_interp, middle_phase, final_phase, final_interp, target_phase.reshape(-1, wd),
    )
    return pl.pallas_call(
        functools.partial(kernel, S, T, N, src_bits, tgt_bits),
        out_shape=pltpu.VMEM((2,) + source_values.shape, F32),
        in_specs=[pl.BlockSpec(memory_space=pltpu.HBM)] * 10,
        out_specs=pl.BlockSpec(memory_space=pltpu.VMEM),
        scratch_shapes=[vm(args[i].shape, args[i].dtype) for i in (0, 3, 4)] + [
            vm((2,) + args[1].shape, F32), vm((3, half, half), BF16), vm((3, R, half), F32), dma((10,)),
            vm((N, 2 * wd, 2 * wd), BF16), vm((wd, 2 * wd), BF16),
            vm((wd, 2 * wd), BF16), vm((wd, 2 * wd), BF16),
            vm((ntab, R, wd), F32), vm((ntab, R, wd), F32),
            vm((S, Q1 * T, wd), SENT), vm((S, Q1 * T, wd), SENT), vm((Q * R, wd), F32),
            vm((T, Q * S, wd), SENT), vm((T, Q * S, wd), SENT), vm((T, Q * S, wd), F32),
            vm((S, T * rhs, wd), BF16),
            vm((S, T * rhs, 2 * wd), BF16), vm((S, T * rhs, 2 * wd), BF16),
            vm((T, S, rhs, wd), BF16), vm((T, S, rhs, wd), BF16),
            dma(()), dma(()), dma(()), dma(()),
            dma(()), dma(()), dma(()), dma(()),
        ],
        compiler_params=pltpu.CompilerParams(
            collective_id=0, has_side_effects=True, vmem_limit_bytes=VLIM
        ),
    )(*[pltpu.with_memory_space_constraint(a, pltpu.HBM) for a in args])


def solution(mesh):
    return jax.shard_map(
        shards,
        mesh=mesh,
        in_specs=(
            P(None, ("src", "tgt")),
            P(("src", "tgt")),
            P(),
            P(),
            P(None, None, ("src", "tgt"), None),
            P(),
            P(None, ("src", "tgt"), None),
            P(("src", "tgt"), None),
            P(),
            P(("src", "tgt")),
        ),
        out_specs=P(None, None, ("src", "tgt")),
        check_vma=False,
    )
```

```python
import functools

import jax
import jax.numpy as jnp
from jax import lax
from jax.experimental import pallas as pl
from jax.experimental.pallas import tpu as pltpu
from jax.sharding import PartitionSpec as P

LOCAL_SRC = 3
LOCAL_TGT = 3
MESH = pl.DeviceIdType.MESH
FIRST = 8
AHEAD = 2
MID_GROUPS = (4,)
FIN_GROUPS = (4,)
VLIM = 40 * 1024 * 1024
F32 = jnp.float32
BF16 = jnp.bfloat16
SENT = jnp.bfloat16
SEG = 64

PI_HI = 3.140625
PI_LO = 9.67653589793e-4
SIN_C = (2.605166276178326e-06, -0.00019809046357444052, 0.008333050617328575, -0.16666657969904702, 0.9999999957158396)
COS_C = (-2.605107617861078e-07, 2.4760135505794177e-05, -0.0013888360842290288, 0.04166663620890442, -0.49999999356955516, 0.9999999997799034)


def cos_sin(x):
    k = lax.round(x * (1.0 / 3.141592653589793), lax.RoundingMethod.TO_NEAREST_EVEN)
    r = (x - k * PI_HI) - k * PI_LO
    z = r * r
    c = jnp.full_like(z, COS_C[0])
    for a in COS_C[1:]:
        c = c * z + a
    s = jnp.full_like(z, SIN_C[0])
    for a in SIN_C[1:]:
        s = s * z + a
    s = s * r
    half = k * 0.5
    odd = jnp.abs(half - lax.round(half, lax.RoundingMethod.TO_NEAREST_EVEN))
    sign = 1.0 - 4.0 * odd
    return c * sign, s * sign


def lane_low(shape, half):
    return lax.broadcasted_iota(jnp.int32, shape, len(shape) - 1) < half


def dup(x):
    return jnp.concatenate([x, x], -1)


def dup_halves(x, half):
    y = pltpu.roll(x, half, x.ndim - 1)
    low = lane_low(x.shape, half)
    return jnp.where(low, x, y), jnp.where(low, y, x)


def xor_rows(x, h):
    rows = x.shape[0]
    up = pltpu.roll(x, rows - h, 0)
    down = pltpu.roll(x, h, 0)
    row = lax.broadcasted_iota(jnp.int32, x.shape, 0)
    return jnp.where((row // h) % 2 == 0, up, down)


def xor_lead(x, h):
    return jnp.concatenate([x[i ^ h : (i ^ h) + 1] for i in range(x.shape[0])], 0)


def xor_index(i, j, size):
    bit = 1
    res = i
    while bit < size:
        if j & bit:
            res = res + bit * (1 - 2 * lax.rem(i // bit, 2))
        bit *= 2
    return res


def encode(x):
    a = jnp.abs(x) * (SEG / 3.141592653589793)
    k = jnp.floor(a)
    v = (1.0 + (a - k)) * jnp.exp2(k - SEG / 2)
    return jnp.where(x < 0, -v, v)


def decode(y):
    u = jnp.abs(y)
    k = jnp.floor(jnp.log2(u))
    r = (k + u * jnp.exp2(-k) + (SEG / 2 - 1)) * (3.141592653589793 / SEG)
    return jnp.where(y < 0, -r, r)


def groups_of(n, sizes):
    at, res = 0, []
    for k in sizes:
        if at < n:
            res.append(tuple(range(at, min(at + k, n))))
            at += k
    while at < n:
        res.append(tuple(range(at, min(at + sizes[-1], n))))
        at += sizes[-1]
    return res


def pairs_of(refs):
    return [(refs[i], refs[min(i + 1, len(refs) - 1)]) for i in range(0, len(refs), 2)]


def kernel(
    S, T, levels, src_bits, tgt_bits,
    values_h, sphase_h, leaf_h, lint_h, lphase_h, mint_h, mphase_h, fphase_h, fint_h, tphase_h,
    out,
    values, lint, lphase, points, mats, phases, in_sem,
    w, wl, wm, wf, tc, ts, ps_out, ph_src, pk2, pk, ph_tgt, pk32, send1, xa, xb, send2, recv2,
    ps_recv, pt_recv, c1_recv, c2_recv,
):
    s_me = lax.axis_index("src")
    t_me = lax.axis_index("tgt")
    half = mats.shape[1]
    wd = 2 * half
    span = T * half
    R = S * T
    rhs = values.shape[0]
    rows = T * rhs
    K = LOCAL_SRC + src_bits
    M = K + tgt_bits
    N = levels

    barrier = pltpu.get_barrier_semaphore()
    for j in range(1, T):
        pl.semaphore_signal(barrier, inc=1, device_id=(s_me, lax.rem(t_me + j, T)), device_id_type=MESH)
    for j in range(1, S):
        pl.semaphore_signal(barrier, inc=1, device_id=(lax.rem(s_me + j, S), t_me), device_id_type=MESH)

    loads = [
        pltpu.make_async_copy(a, b, in_sem.at[i])
        for a, b, i in (
            (sphase_h, points.at[0], 0), (tphase_h, points.at[1], 0),
            (lphase_h.at[0:K, :, 0:T], lphase.at[0:K, :, 0:T], 3),
            (values_h.at[:, 0:span], values.at[:, 0:span], 2),
            (leaf_h, mats.at[0], 1),
            (lint_h.at[0:LOCAL_SRC], lint.at[0:LOCAL_SRC], 4),
            (mint_h, mats.at[1], 1), (fint_h, mats.at[2], 1),
            (values_h.at[:, span : S * span], values.at[:, span : S * span], 0),
            (lphase_h.at[0:K, :, T:R], lphase.at[0:K, :, T:R], 1),
            (lphase_h.at[K:N], lphase.at[K:N], 2),
            (mphase_h, phases.at[0:2], 5), (fphase_h, phases.at[2], 5),
            (lint_h.at[LOCAL_SRC:N], lint.at[LOCAL_SRC:N], 6),
        )
    ]
    both_points = pltpu.make_async_copy(points, points, in_sem.at[0])
    all_mats = pltpu.make_async_copy(mats, mats, in_sem.at[1])
    all_phases = pltpu.make_async_copy(phases, phases, in_sem.at[5])
    ps_send, c1_send, pt_send, c2_send = (in_sem.at[i] for i in (3, 4, 5, 6))
    for load in loads[:FIRST]:
        load.start()

    low = lane_low((R, wd), half)

    def put(idx, angle, at=0):
        n = angle.shape[0]
        c, s = cos_sin(angle)
        tc[idx, at : at + n] = c
        ts[idx, at : at + n] = jnp.where(low[:n], -s, s)

    def put_two(ia, ib, packed, at=0):
        n = packed.shape[0]
        m = low[:n]
        c, s = cos_sin(packed)
        cr = pltpu.roll(c, half, 1)
        sr = pltpu.roll(s, half, 1)
        tc[ia, at : at + n] = jnp.where(m, c, cr)
        tc[ib, at : at + n] = jnp.where(m, cr, c)
        ts[ia, at : at + n] = jnp.where(m, -s, sr)
        ts[ib, at : at + n] = jnp.where(m, -sr, s)

    def put_level(n, prev, pair, h, at=0):
        packed = jnp.where(low[: pair.shape[0]], pair, xor_rows(pair, h))
        put_two(2 * n, 2 * n + 1, packed if prev is None else prev + packed, at)

    def both(a, b):
        return jnp.concatenate([a, b], -1)

    def lpair(n, a=0, b=R):
        return both(lphase[n, 0, a:b], lphase[n, 1, a:b])

    def lp(n, q, a=0, b=R):
        return dup(lphase[n, q, a:b])

    I_SEND1, I_MID, I_FIN, I_TGT, I_SRC = (2 * N + i for i in range(5))

    def point_rows(ref):
        lo, hi = dup_halves(ref[...], half)
        n = lo.shape[0]
        return jnp.concatenate([jnp.concatenate([lo[i : i + 1], hi[i : i + 1]], 0) for i in range(n)], 0)

    def fill(dst, r, L):
        z = jnp.zeros_like(L)
        lz = jnp.concatenate([L, z], 1)
        zl = jnp.concatenate([z, L], 1)
        dst[r : r + half, 0:wd] = lz
        dst[r : r + half, wd : 2 * wd] = zl
        dst[r + half : r + wd, 0:wd] = zl
        dst[r + half : r + wd, wd : 2 * wd] = lz

    def blk(i):
        return pl.ds(pl.multiple_of(i * T, T), T)

    def ps_copy(e):
        return pltpu.make_async_remote_copy(
            src_ref=ps_out.at[e], dst_ref=ph_src.at[s_me],
            send_sem=ps_send, recv_sem=ps_recv, device_id=(e, t_me), device_id_type=MESH,
        )

    def pt_copy(j):
        e = xor_index(t_me, j, T)
        return pltpu.make_async_remote_copy(
            src_ref=pk.at[e], dst_ref=ph_tgt.at[t_me],
            send_sem=pt_send, recv_sem=pt_recv, device_id=(s_me, e), device_id_type=MESH,
        )

    def c1_copy(e):
        return pltpu.make_async_remote_copy(
            src_ref=send1.at[e], dst_ref=xa.at[s_me, :, pl.ds(0, wd)],
            send_sem=c1_send, recv_sem=c1_recv, device_id=(e, t_me), device_id_type=MESH,
        )

    def c2_copy(k):
        e = k + (t_me <= k).astype(jnp.int32)
        return pltpu.make_async_remote_copy(
            src_ref=send2.at[e], dst_ref=recv2.at[t_me],
            send_sem=c2_send, recv_sem=c2_recv, device_id=(s_me, e), device_id_type=MESH,
        )

    def pt_start():
        for j in range(T - 1, 0, -1):
            pt_copy(j).start()

    s_one = (xor_index(s_me, 1, S), t_me)
    t_one = (s_me, xor_index(t_me, 1, T))
    ps_all = pltpu.make_async_remote_copy(
        src_ref=ps_out.at[pl.ds(0, S - 1)], dst_ref=ph_src.at[pl.ds(0, S - 1)],
        send_sem=ps_send, recv_sem=ps_recv, device_id=s_one, device_id_type=MESH,
    )
    pt_all = pltpu.make_async_remote_copy(
        src_ref=pk.at[pl.ds(0, T - 1)], dst_ref=ph_tgt.at[pl.ds(0, T - 1)],
        send_sem=pt_send, recv_sem=pt_recv, device_id=t_one, device_id_type=MESH,
    )
    c1_all = pltpu.make_async_remote_copy(
        src_ref=send1.at[pl.ds(0, S - 1)], dst_ref=xa.at[pl.ds(0, S - 1), :, pl.ds(0, wd)],
        send_sem=c1_send, recv_sem=c1_recv, device_id=s_one, device_id_type=MESH,
    )

    c2_all = pltpu.make_async_remote_copy(
        src_ref=send2.at[pl.ds(0, T - 1)], dst_ref=recv2.at[pl.ds(0, T - 1)],
        send_sem=c2_send, recv_sem=c2_recv, device_id=t_one, device_id_type=MESH,
    )

    def spread(table, idx, i):
        return jnp.stack([table[idx, pl.ds(i * T + t, 8, stride=0), :] for t in range(T)], 0)

    def tab(idx, i):
        return spread(tc, idx, i), spread(ts, idx, i)

    def split(y):
        y = y.reshape(T, rhs, 2 * wd)
        return y[:, :, :wd], y[:, :, wd:]

    def rot(v, sw, idx, i):
        c, s = tab(idx, i)
        return jnp.concatenate([v[:, r : r + 8] * c + sw[:, r : r + 8] * s for r in range(0, rhs, 8)], 1)

    def dot(x, m):
        return jnp.dot(x, m, preferred_element_type=F32)

    def step(v, sw, n, i, h):
        own = rot(v, sw, 2 * n, i).astype(BF16)
        oth = xor_lead(rot(v, sw, 2 * n + 1, i), h).astype(BF16)
        x = jnp.concatenate([own, oth], -1).reshape(rows, 2 * wd)
        return split(dot(x, w[n]))

    def last_step(v, sw, n, i, h):
        own = rot(v, sw, 2 * n, i).astype(BF16)
        oth = xor_lead(rot(v, sw, 2 * n + 1, i), h).astype(BF16)
        x = jnp.concatenate([own, oth], -1).reshape(rows, 2 * wd)
        return dot(x, w[n, :, :wd]).reshape(T, rhs, wd)

    both_points.wait()
    all_mats.wait()
    loads[3].wait()
    for load in loads[FIRST:]:
        load.start()
    c, s = cos_sin(point_rows(points.at[0]))
    tc[I_SRC] = jnp.where(lane_low(c.shape, half), c, -s)
    fill(wl, 0, mats[0])
    def leaf_part(e):
        parts = []
        for p in range(T // 2):
            parts.extend(dup_halves(values[:, e * span + p * wd : e * span + (p + 1) * wd], half))
        c = spread(tc, I_SRC, e)
        x = jnp.stack(parts, 0)
        x = jnp.concatenate([x[:, r : r + 8] * c for r in range(0, rhs, 8)], 1)
        return x.astype(BF16).reshape(rows, wd)

    xb[0, :, :wd] = leaf_part(0)

    loads[2].wait()
    loads[5].wait()

    src_pairs = [(lphase.at[n, 0], lphase.at[n, 1]) for n in range(LOCAL_SRC, K)]
    src_pairs += pairs_of([lphase.at[n, 2] for n in range(LOCAL_SRC, K)])
    tgt_pairs = [(phases.at[0], phases.at[1])]
    tgt_pairs += [(lphase.at[n, 0], lphase.at[n, 1]) for n in range(K, M)]
    tgt_pairs += pairs_of([lphase.at[n, 2] for n in range(K, M - 1)])
    Q = len(tgt_pairs)

    def src_part(blocks):
        a, b = blocks[0] * T, blocks[-1] * T + T
        state = [split(dot(xb[e, :, :wd], wl[...])) for e in blocks]
        for n in range(LOCAL_SRC):
            put_level(n, None if n == 0 else lp(n - 1, 2, a, b), lpair(n, a, b), 2**n, a)
            if blocks[0] == 0:
                fill(w.at[n], 0, lint[n, 0])
                fill(w.at[n], 2 * half, lint[n, 1])
            state = [step(v, sw, n, e, 2**n) for e, (v, sw) in zip(blocks, state)]
        put(I_SEND1, lp(LOCAL_SRC - 1, 2, a, b) + lp(LOCAL_SRC, 0, a, b), a)
        for e, (v, sw) in zip(blocks, state):
            send1[e] = rot(v, sw, I_SEND1, e).astype(BF16).reshape(rows, wd)

    def pack_src(blocks):
        for q, (a, b) in enumerate(src_pairs):
            for e in blocks:
                at = slice(e * T, (e + 1) * T)
                ps_out[e, q * T : (q + 1) * T, :] = encode(both(a[at], b[at])).astype(SENT)

    def pack_tgt():
        for q, (a, b) in enumerate(tgt_pairs):
            pk2[q * R : (q + 1) * R, :] = both(a[...], b[...])
        for d in range(T):
            pk[d] = encode(pk2[pl.ds(d, Q * S, stride=T), :]).astype(SENT)

    pack_src([0])

    def wait_rest():
        loads[8].wait()
        loads[9].wait()

    def pack_rest():
        loads[10].wait()
        all_phases.wait()
        pack_tgt()

    @pl.when(s_me == 0)
    def _():
        wait_rest()
        pack_rest()

    rest = list(range(1, S))

    def src_rest():
        for e in rest:
            xb[e, :, :wd] = leaf_part(e)
        pack_src(rest)
        src_part(rest)

    block_ahead = t_me < T // 2
    all_ahead = t_me < T // 4

    @pl.when(block_ahead)
    def _():
        src_part([0])

    @pl.when(all_ahead & (s_me != 0))
    def _():
        wait_rest()

    @pl.when(all_ahead)
    def _():
        src_rest()

    pl.semaphore_wait(barrier, S - 1 + T - 1)

    @pl.when(s_me != 0)
    def _():
        ps_copy(0).start()

    @pl.when(s_me == 0)
    def _():
        pt_start()

    @pl.when(jnp.logical_not(block_ahead))
    def _():
        src_part([0])

    @pl.when(s_me != 0)
    def _():
        c1_copy(0).start()

        @pl.when(jnp.logical_not(all_ahead))
        def _():
            wait_rest()

        pack_rest()
        pt_start()

    @pl.when(jnp.logical_not(all_ahead))
    def _():
        src_rest()

    def others_start():
        for e in rest:
            @pl.when(s_me != e)
            def _():
                ps_copy(e).start()
                c1_copy(e).start()

    @pl.when(s_me != 0)
    def _():
        others_start()

    xa[s_me, :, :wd] = send1[s_me]

    loads[13].wait()
    for n in range(LOCAL_SRC, M):
        fill(w.at[n], 0, lint[n, 0])
        fill(w.at[n], 2 * half, lint[n, 1])
    fill(wm, 0, mats[1])
    ph_src[s_me] = ps_out[s_me]
    ph_tgt[t_me] = pk[t_me]

    @pl.when(s_me == 0)
    def _():
        others_start()

    ps_all.wait_recv()
    got = [decode(ph_src[i].astype(F32)) for i in range(S)]
    sang = [jnp.concatenate([x[q * T : (q + 1) * T] for x in got], 0) for q in range(len(src_pairs))]
    sres = []
    for q in range(src_bits, len(src_pairs)):
        sres.extend(dup_halves(sang[q], half))
    own, oth = dup_halves(sang[0], half)
    put(2 * LOCAL_SRC + 1, xor_rows(oth, T) - own)
    for b in range(1, src_bits):
        put_level(LOCAL_SRC + b, sres[b - 1], sang[b], T * 2**b)
    pt_all.wait_recv()
    for d in range(T):
        pk32[d] = decode(ph_tgt[d].astype(F32))
    tang = [jnp.concatenate([pk32[:, q * S + i, :] for i in range(S)], 0) for q in range(Q)]
    mid0, mid1 = dup_halves(tang[0], half)
    tres = [mid1]
    for q in range(1 + tgt_bits, Q):
        tres.extend(dup_halves(tang[q], half))
    put(I_MID, sres[src_bits - 1] + mid0)
    for b in range(tgt_bits):
        put_level(K + b, tres[b], tang[1 + b], 2**b)
    c1_all.wait_recv()
    bufs = (xa, xb)
    for b in range(src_bits):
        n = LOCAL_SRC + b
        dst = bufs[b % 2]
        for i in range(S):
            if b == 0:
                v = xa[i, :, :wd].astype(F32).reshape(T, rhs, wd)
                sw = pltpu.roll(v, half, 2)
            else:
                v, sw = split(dot(bufs[(b - 1) % 2][i], w[n - 1]))
                dst[i, :, :wd] = rot(v, sw, 2 * n, i).astype(BF16).reshape(rows, wd)
            dst[i ^ 2**b, :, wd:] = rot(v, sw, 2 * n + 1, i).astype(BF16).reshape(rows, wd)

    for blocks in groups_of(S, MID_GROUPS):
        state = [split(dot(bufs[(src_bits - 1) % 2][i], w[K - 1])) for i in blocks]
        state = [rot(v, sw, I_MID, i).astype(BF16).reshape(rows, wd) for i, (v, sw) in zip(blocks, state)]
        state = [split(dot(x, wm[...])) for x in state]
        for b in range(tgt_bits):
            if b < tgt_bits - 1:
                state = [step(v, sw, K + b, i, 2**b) for i, (v, sw) in zip(blocks, state)]
            else:
                state = [last_step(v, sw, K + b, i, 2**b) for i, (v, sw) in zip(blocks, state)]
        for i, v in zip(blocks, state):
            send2[:, i] = v.astype(BF16)
    for k in range(AHEAD):
        c2_copy(k).start()
    for n in range(M, N):
        fill(w.at[n], 0, lint[n, 0])
        fill(w.at[n], 2 * half, lint[n, 1])
    fill(wf, 0, mats[2])
    for n in range(M, N):
        put_level(n, lp(n - 1, 2), lpair(n), 2 ** (n - M))
    put(I_FIN, lp(N - 1, 2) + dup(phases[2]))
    c, s = cos_sin(points[1])
    tc[I_TGT, 0 : R // 2] = c
    ts[I_TGT, 0 : R // 2] = s
    for k in range(AHEAD, T - 1):
        c2_copy(k).start()
    recv2[t_me] = send2[t_me]

    low3 = lane_low((rhs, wd), half)

    c2_all.wait_recv()
    for blocks in groups_of(S, FIN_GROUPS):
        state = []
        for i in blocks:
            v = recv2[:, i].astype(F32)
            state.append((v, pltpu.roll(v, half, 2)))
        for n in range(M, N):
            state = [step(v, sw, n, i, 2 ** (n - M)) for i, (v, sw) in zip(blocks, state)]
        state = [rot(v, sw, I_FIN, i).astype(BF16).reshape(rows, wd) for i, (v, sw) in zip(blocks, state)]
        state = [split(dot(x, wf[...])) for x in state]
        for i, (v, sw) in zip(blocks, state):
            for p in range(T // 2):
                row = pl.ds(i * (T // 2) + p, 8, stride=0)
                c = jnp.concatenate([tc[I_TGT, row, :]] * (rhs // 8), 0)
                s = jnp.concatenate([ts[I_TGT, row, :]] * (rhs // 8), 0)
                re = jnp.where(low3, v[2 * p], sw[2 * p + 1])
                im = jnp.where(low3, sw[2 * p], v[2 * p + 1])
                col = pl.ds(i * T * half + p * wd, wd)
                out[0, :, col] = re * c - im * s
                out[1, :, col] = re * s + im * c
    ps_all.wait_send()
    pt_all.wait_send()
    c1_all.wait_send()
    c2_all.wait_send()


def shards(
    source_values, source_phase, leaf_interp, level_interp, level_phase,
    middle_interp, middle_phase, final_phase, final_interp, target_phase,
):
    S = lax.axis_size("src")
    T = lax.axis_size("tgt")
    R = level_phase.shape[2]
    assert R == S * T
    rhs = source_values.shape[0]
    half = leaf_interp.shape[1]
    wd = 2 * half
    N = level_phase.shape[0]
    src_bits = S.bit_length() - 1
    tgt_bits = T.bit_length() - 1
    assert N == LOCAL_SRC + src_bits + tgt_bits + LOCAL_TGT
    Q1 = src_bits + (src_bits + 1) // 2
    Q = 1 + tgt_bits + tgt_bits // 2
    ntab = 2 * N + 5
    vm = pltpu.VMEM
    dma = pltpu.SemaphoreType.DMA
    args = (
        source_values, source_phase.reshape(-1, wd), leaf_interp, level_interp, level_phase,
        middle_interp, middle_phase, final_phase, final_interp, target_phase.reshape(-1, wd),
    )
    return pl.pallas_call(
        functools.partial(kernel, S, T, N, src_bits, tgt_bits),
        out_shape=pltpu.VMEM((2,) + source_values.shape, F32),
        in_specs=[pl.BlockSpec(memory_space=pltpu.HBM)] * 10,
        out_specs=pl.BlockSpec(memory_space=pltpu.VMEM),
        scratch_shapes=[vm(args[i].shape, args[i].dtype) for i in (0, 3, 4)] + [
            vm((2,) + args[1].shape, F32), vm((3, half, half), BF16), vm((3, R, half), F32), dma((7,)),
            vm((N, 2 * wd, 2 * wd), BF16), vm((wd, 2 * wd), BF16),
            vm((wd, 2 * wd), BF16), vm((wd, 2 * wd), BF16),
            vm((ntab, R, wd), F32), vm((ntab, R, wd), F32),
            vm((S, Q1 * T, wd), SENT), vm((S, Q1 * T, wd), SENT), vm((Q * R, wd), F32),
            vm((T, Q * S, wd), SENT), vm((T, Q * S, wd), SENT), vm((T, Q * S, wd), F32),
            vm((S, T * rhs, wd), BF16),
            vm((S, T * rhs, 2 * wd), BF16), vm((S, T * rhs, 2 * wd), BF16),
            vm((T, S, rhs, wd), BF16), vm((T, S, rhs, wd), BF16),
            dma(()), dma(()), dma(()), dma(()),
        ],
        compiler_params=pltpu.CompilerParams(
            collective_id=0, has_side_effects=True, vmem_limit_bytes=VLIM
        ),
    )(*[pltpu.with_memory_space_constraint(a, pltpu.HBM) for a in args])


def solution(mesh):
    return jax.shard_map(
        shards,
        mesh=mesh,
        in_specs=(
            P(None, ("src", "tgt")),
            P(("src", "tgt")),
            P(),
            P(),
            P(None, None, ("src", "tgt"), None),
            P(),
            P(None, ("src", "tgt"), None),
            P(("src", "tgt"), None),
            P(),
            P(("src", "tgt")),
        ),
        out_specs=P(None, None, ("src", "tgt")),
        check_vma=False,
    )
```

```python
import functools

import jax
import jax.numpy as jnp
from jax import lax
from jax.experimental import pallas as pl
from jax.experimental.pallas import tpu as pltpu
from jax.sharding import PartitionSpec as P

LOCAL_SRC = 3
LOCAL_TGT = 3
MESH = pl.DeviceIdType.MESH
FIRST = 8
AHEAD = 2
MID_GROUPS = (4,)
FIN_GROUPS = (4,)
VLIM = 40 * 1024 * 1024
F32 = jnp.float32
BF16 = jnp.bfloat16
SENT = jnp.bfloat16
SEG = 64

PI_HI = 3.140625
PI_LO = 9.67653589793e-4
SIN_C = (2.605166276178326e-06, -0.00019809046357444052, 0.008333050617328575, -0.16666657969904702, 0.9999999957158396)
COS_C = (-2.605107617861078e-07, 2.4760135505794177e-05, -0.0013888360842290288, 0.04166663620890442, -0.49999999356955516, 0.9999999997799034)


def cos_sin(x):
    k = lax.round(x * (1.0 / 3.141592653589793), lax.RoundingMethod.TO_NEAREST_EVEN)
    r = (x - k * PI_HI) - k * PI_LO
    z = r * r
    c = jnp.full_like(z, COS_C[0])
    for a in COS_C[1:]:
        c = c * z + a
    s = jnp.full_like(z, SIN_C[0])
    for a in SIN_C[1:]:
        s = s * z + a
    s = s * r
    half = k * 0.5
    odd = jnp.abs(half - lax.round(half, lax.RoundingMethod.TO_NEAREST_EVEN))
    sign = 1.0 - 4.0 * odd
    return c * sign, s * sign


def lane_low(shape, half):
    return lax.broadcasted_iota(jnp.int32, shape, len(shape) - 1) < half


def dup(x):
    return jnp.concatenate([x, x], -1)


def dup_halves(x, half):
    y = pltpu.roll(x, half, x.ndim - 1)
    low = lane_low(x.shape, half)
    return jnp.where(low, x, y), jnp.where(low, y, x)


def xor_rows(x, h):
    rows = x.shape[0]
    up = pltpu.roll(x, rows - h, 0)
    down = pltpu.roll(x, h, 0)
    row = lax.broadcasted_iota(jnp.int32, x.shape, 0)
    return jnp.where((row // h) % 2 == 0, up, down)


def xor_lead(x, h):
    return jnp.concatenate([x[i ^ h : (i ^ h) + 1] for i in range(x.shape[0])], 0)


def xor_index(i, j, size):
    bit = 1
    res = i
    while bit < size:
        if j & bit:
            res = res + bit * (1 - 2 * lax.rem(i // bit, 2))
        bit *= 2
    return res


def encode(x):
    a = jnp.abs(x) * (SEG / 3.141592653589793)
    k = jnp.floor(a)
    v = (1.0 + (a - k)) * jnp.exp2(k - SEG / 2)
    return jnp.where(x < 0, -v, v)


def decode(y):
    u = jnp.abs(y)
    k = jnp.floor(jnp.log2(u))
    r = (k + u * jnp.exp2(-k) + (SEG / 2 - 1)) * (3.141592653589793 / SEG)
    return jnp.where(y < 0, -r, r)


def groups_of(n, sizes):
    at, res = 0, []
    for k in sizes:
        if at < n:
            res.append(tuple(range(at, min(at + k, n))))
            at += k
    while at < n:
        res.append(tuple(range(at, min(at + sizes[-1], n))))
        at += sizes[-1]
    return res


def pairs_of(refs):
    return [(refs[i], refs[min(i + 1, len(refs) - 1)]) for i in range(0, len(refs), 2)]


def kernel(
    S, T, levels, src_bits, tgt_bits,
    values_h, sphase_h, leaf_h, lint_h, lphase_h, mint_h, mphase_h, fphase_h, fint_h, tphase_h,
    out,
    values, lint, lphase, points, mats, phases, in_sem,
    w, wl, wm, wf, tc, ts, ps_out, ph_src, pk2, pk, ph_tgt, pk32, send1, xa, xb, send2, recv2,
    ps_recv, pt_recv, c1_recv, c2_recv,
):
    s_me = lax.axis_index("src")
    t_me = lax.axis_index("tgt")
    half = mats.shape[1]
    wd = 2 * half
    span = T * half
    R = S * T
    rhs = values.shape[0]
    rows = T * rhs
    K = LOCAL_SRC + src_bits
    M = K + tgt_bits
    N = levels

    barrier = pltpu.get_barrier_semaphore()
    for j in range(1, T):
        pl.semaphore_signal(barrier, inc=1, device_id=(s_me, lax.rem(t_me + j, T)), device_id_type=MESH)
    for j in range(1, S):
        pl.semaphore_signal(barrier, inc=1, device_id=(lax.rem(s_me + j, S), t_me), device_id_type=MESH)

    loads = [
        pltpu.make_async_copy(a, b, in_sem.at[i])
        for a, b, i in (
            (sphase_h, points.at[0], 0), (tphase_h, points.at[1], 0),
            (lphase_h.at[0:K, :, 0:T], lphase.at[0:K, :, 0:T], 3),
            (values_h.at[:, 0:span], values.at[:, 0:span], 2),
            (leaf_h, mats.at[0], 1),
            (lint_h.at[0:LOCAL_SRC], lint.at[0:LOCAL_SRC], 4),
            (mint_h, mats.at[1], 1), (fint_h, mats.at[2], 1),
            (values_h.at[:, span : S * span], values.at[:, span : S * span], 0),
            (lphase_h.at[0:K, :, T:R], lphase.at[0:K, :, T:R], 1),
            (lphase_h.at[K:N], lphase.at[K:N], 2),
            (mphase_h, phases.at[0:2], 5), (fphase_h, phases.at[2], 5),
            (lint_h.at[LOCAL_SRC:N], lint.at[LOCAL_SRC:N], 6),
        )
    ]
    both_points = pltpu.make_async_copy(points, points, in_sem.at[0])
    all_mats = pltpu.make_async_copy(mats, mats, in_sem.at[1])
    all_phases = pltpu.make_async_copy(phases, phases, in_sem.at[5])
    ps_send, c1_send, pt_send, c2_send = (in_sem.at[i] for i in (3, 4, 5, 6))
    for load in loads[:FIRST]:
        load.start()

    low = lane_low((R, wd), half)

    def put(idx, angle, at=0):
        n = angle.shape[0]
        c, s = cos_sin(angle)
        tc[idx, at : at + n] = c
        ts[idx, at : at + n] = jnp.where(low[:n], -s, s)

    def put_two(ia, ib, packed, at=0):
        n = packed.shape[0]
        m = low[:n]
        c, s = cos_sin(packed)
        cr = pltpu.roll(c, half, 1)
        sr = pltpu.roll(s, half, 1)
        tc[ia, at : at + n] = jnp.where(m, c, cr)
        tc[ib, at : at + n] = jnp.where(m, cr, c)
        ts[ia, at : at + n] = jnp.where(m, -s, sr)
        ts[ib, at : at + n] = jnp.where(m, -sr, s)

    def put_level(n, prev, pair, h, at=0):
        packed = jnp.where(low[: pair.shape[0]], pair, xor_rows(pair, h))
        put_two(2 * n, 2 * n + 1, packed if prev is None else prev + packed, at)

    def both(a, b):
        return jnp.concatenate([a, b], -1)

    def lpair(n, a=0, b=R):
        return both(lphase[n, 0, a:b], lphase[n, 1, a:b])

    def lp(n, q, a=0, b=R):
        return dup(lphase[n, q, a:b])

    I_SEND1, I_MID, I_FIN, I_TGT, I_SRC = (2 * N + i for i in range(5))

    def point_rows(ref):
        lo, hi = dup_halves(ref[...], half)
        n = lo.shape[0]
        return jnp.concatenate([jnp.concatenate([lo[i : i + 1], hi[i : i + 1]], 0) for i in range(n)], 0)

    def fill(dst, r, L):
        z = jnp.zeros_like(L)
        lz = jnp.concatenate([L, z], 1)
        zl = jnp.concatenate([z, L], 1)
        dst[r : r + half, 0:wd] = lz
        dst[r : r + half, wd : 2 * wd] = zl
        dst[r + half : r + wd, 0:wd] = zl
        dst[r + half : r + wd, wd : 2 * wd] = lz

    def blk(i):
        return pl.ds(pl.multiple_of(i * T, T), T)

    def ps_copy(e):
        return pltpu.make_async_remote_copy(
            src_ref=ps_out.at[e], dst_ref=ph_src.at[s_me],
            send_sem=ps_send, recv_sem=ps_recv, device_id=(e, t_me), device_id_type=MESH,
        )

    def pt_copy(j):
        e = xor_index(t_me, j, T)
        return pltpu.make_async_remote_copy(
            src_ref=pk.at[e], dst_ref=ph_tgt.at[t_me],
            send_sem=pt_send, recv_sem=pt_recv, device_id=(s_me, e), device_id_type=MESH,
        )

    def c1_copy(e):
        return pltpu.make_async_remote_copy(
            src_ref=send1.at[e], dst_ref=xa.at[s_me, :, pl.ds(0, wd)],
            send_sem=c1_send, recv_sem=c1_recv, device_id=(e, t_me), device_id_type=MESH,
        )

    def c2_copy(k):
        e = k + (t_me <= k).astype(jnp.int32)
        return pltpu.make_async_remote_copy(
            src_ref=send2.at[e], dst_ref=recv2.at[t_me],
            send_sem=c2_send, recv_sem=c2_recv, device_id=(s_me, e), device_id_type=MESH,
        )

    def pt_start():
        for j in range(T - 1, 0, -1):
            pt_copy(j).start()

    s_one = (xor_index(s_me, 1, S), t_me)
    t_one = (s_me, xor_index(t_me, 1, T))
    ps_all = pltpu.make_async_remote_copy(
        src_ref=ps_out.at[pl.ds(0, S - 1)], dst_ref=ph_src.at[pl.ds(0, S - 1)],
        send_sem=ps_send, recv_sem=ps_recv, device_id=s_one, device_id_type=MESH,
    )
    pt_all = pltpu.make_async_remote_copy(
        src_ref=pk.at[pl.ds(0, T - 1)], dst_ref=ph_tgt.at[pl.ds(0, T - 1)],
        send_sem=pt_send, recv_sem=pt_recv, device_id=t_one, device_id_type=MESH,
    )
    c1_all = pltpu.make_async_remote_copy(
        src_ref=send1.at[pl.ds(0, S - 1)], dst_ref=xa.at[pl.ds(0, S - 1), :, pl.ds(0, wd)],
        send_sem=c1_send, recv_sem=c1_recv, device_id=s_one, device_id_type=MESH,
    )

    c2_all = pltpu.make_async_remote_copy(
        src_ref=send2.at[pl.ds(0, T - 1)], dst_ref=recv2.at[pl.ds(0, T - 1)],
        send_sem=c2_send, recv_sem=c2_recv, device_id=t_one, device_id_type=MESH,
    )

    def spread(table, idx, i):
        return jnp.stack([table[idx, pl.ds(i * T + t, 8, stride=0), :] for t in range(T)], 0)

    def tab(idx, i):
        return spread(tc, idx, i), spread(ts, idx, i)

    def split(y):
        y = y.reshape(T, rhs, 2 * wd)
        return y[:, :, :wd], y[:, :, wd:]

    def rot(v, sw, idx, i):
        c, s = tab(idx, i)
        return jnp.concatenate([v[:, r : r + 8] * c + sw[:, r : r + 8] * s for r in range(0, rhs, 8)], 1)

    def dot(x, m):
        return jnp.dot(x, m, preferred_element_type=F32)

    def step(v, sw, n, i, h):
        own = rot(v, sw, 2 * n, i).astype(BF16)
        oth = xor_lead(rot(v, sw, 2 * n + 1, i), h).astype(BF16)
        x = jnp.concatenate([own, oth], -1).reshape(rows, 2 * wd)
        return split(dot(x, w[n]))

    def last_step(v, sw, n, i, h):
        own = rot(v, sw, 2 * n, i).astype(BF16)
        oth = xor_lead(rot(v, sw, 2 * n + 1, i), h).astype(BF16)
        x = jnp.concatenate([own, oth], -1).reshape(rows, 2 * wd)
        return dot(x, w[n, :, :wd]).reshape(T, rhs, wd)

    both_points.wait()
    all_mats.wait()
    loads[3].wait()
    for load in loads[FIRST:]:
        load.start()
    c, s = cos_sin(point_rows(points.at[0]))
    tc[I_SRC] = jnp.where(lane_low(c.shape, half), c, -s)
    fill(wl, 0, mats[0])
    def leaf_part(e):
        parts = []
        for p in range(T // 2):
            parts.extend(dup_halves(values[:, e * span + p * wd : e * span + (p + 1) * wd], half))
        c = spread(tc, I_SRC, e)
        x = jnp.stack(parts, 0)
        x = jnp.concatenate([x[:, r : r + 8] * c for r in range(0, rhs, 8)], 1)
        return x.astype(BF16).reshape(rows, wd)

    xb[0, :, :wd] = leaf_part(0)

    loads[2].wait()
    loads[5].wait()

    src_pairs = [(lphase.at[n, 0], lphase.at[n, 1]) for n in range(LOCAL_SRC, K)]
    src_pairs += pairs_of([lphase.at[n, 2] for n in range(LOCAL_SRC, K)])
    tgt_pairs = [(phases.at[0], phases.at[1])]
    tgt_pairs += [(lphase.at[n, 0], lphase.at[n, 1]) for n in range(K, M)]
    tgt_pairs += pairs_of([lphase.at[n, 2] for n in range(K, M - 1)])
    Q = len(tgt_pairs)

    def src_part(blocks):
        a, b = blocks[0] * T, blocks[-1] * T + T
        state = [split(dot(xb[e, :, :wd], wl[...])) for e in blocks]
        for n in range(LOCAL_SRC):
            put_level(n, None if n == 0 else lp(n - 1, 2, a, b), lpair(n, a, b), 2**n, a)
            if blocks[0] == 0:
                fill(w.at[n], 0, lint[n, 0])
                fill(w.at[n], 2 * half, lint[n, 1])
            state = [step(v, sw, n, e, 2**n) for e, (v, sw) in zip(blocks, state)]
        put(I_SEND1, lp(LOCAL_SRC - 1, 2, a, b) + lp(LOCAL_SRC, 0, a, b), a)
        for e, (v, sw) in zip(blocks, state):
            send1[e] = rot(v, sw, I_SEND1, e).astype(BF16).reshape(rows, wd)

    def pack_src(blocks):
        for q, (a, b) in enumerate(src_pairs):
            for e in blocks:
                at = slice(e * T, (e + 1) * T)
                ps_out[e, q * T : (q + 1) * T, :] = encode(both(a[at], b[at])).astype(SENT)

    def pack_tgt():
        for q, (a, b) in enumerate(tgt_pairs):
            pk2[q * R : (q + 1) * R, :] = both(a[...], b[...])
        for d in range(T):
            pk[d] = encode(pk2[pl.ds(d, Q * S, stride=T), :]).astype(SENT)

    pack_src([0])

    def wait_rest():
        loads[8].wait()
        loads[9].wait()

    def pack_rest():
        loads[10].wait()
        all_phases.wait()
        pack_tgt()

    @pl.when(s_me == 0)
    def _():
        wait_rest()
        pack_rest()

    rest = list(range(1, S))

    def src_rest():
        for e in rest:
            xb[e, :, :wd] = leaf_part(e)
        pack_src(rest)
        src_part(rest)

    block_ahead = t_me < T // 2
    all_ahead = t_me < T // 4

    @pl.when(block_ahead)
    def _():
        src_part([0])

    @pl.when(all_ahead & (s_me != 0))
    def _():
        wait_rest()

    @pl.when(all_ahead)
    def _():
        src_rest()

    pl.semaphore_wait(barrier, S - 1 + T - 1)

    @pl.when(s_me != 0)
    def _():
        ps_copy(0).start()

    @pl.when(s_me == 0)
    def _():
        pt_start()

    @pl.when(jnp.logical_not(block_ahead))
    def _():
        src_part([0])

    @pl.when(s_me != 0)
    def _():
        c1_copy(0).start()

        @pl.when(jnp.logical_not(all_ahead))
        def _():
            wait_rest()

        pack_rest()
        pt_start()

    @pl.when(jnp.logical_not(all_ahead))
    def _():
        src_rest()

    def others_start():
        for e in rest:
            @pl.when(s_me != e)
            def _():
                ps_copy(e).start()
                c1_copy(e).start()

    @pl.when(s_me != 0)
    def _():
        others_start()

    xa[s_me, :, :wd] = send1[s_me]

    loads[13].wait()
    for n in range(LOCAL_SRC, M):
        fill(w.at[n], 0, lint[n, 0])
        fill(w.at[n], 2 * half, lint[n, 1])
    fill(wm, 0, mats[1])
    ph_src[s_me] = ps_out[s_me]
    ph_tgt[t_me] = pk[t_me]

    @pl.when(s_me == 0)
    def _():
        others_start()

    ps_all.wait_recv()
    got = [decode(ph_src[i].astype(F32)) for i in range(S)]
    sang = [jnp.concatenate([x[q * T : (q + 1) * T] for x in got], 0) for q in range(len(src_pairs))]
    sres = []
    for q in range(src_bits, len(src_pairs)):
        sres.extend(dup_halves(sang[q], half))
    own, oth = dup_halves(sang[0], half)
    put(2 * LOCAL_SRC + 1, xor_rows(oth, T) - own)
    for b in range(1, src_bits):
        put_level(LOCAL_SRC + b, sres[b - 1], sang[b], T * 2**b)
    pt_all.wait_recv()
    for d in range(T):
        pk32[d] = decode(ph_tgt[d].astype(F32))
    tang = [jnp.concatenate([pk32[:, q * S + i, :] for i in range(S)], 0) for q in range(Q)]
    mid0, mid1 = dup_halves(tang[0], half)
    tres = [mid1]
    for q in range(1 + tgt_bits, Q):
        tres.extend(dup_halves(tang[q], half))
    put(I_MID, sres[src_bits - 1] + mid0)
    for b in range(tgt_bits):
        put_level(K + b, tres[b], tang[1 + b], 2**b)
    c1_all.wait_recv()
    bufs = (xa, xb)
    for b in range(src_bits):
        n = LOCAL_SRC + b
        dst = bufs[b % 2]
        for i in range(S):
            if b == 0:
                v = xa[i, :, :wd]
                v, sw = (x.astype(F32).reshape(T, rhs, wd) for x in (v, pltpu.roll(v, half, 1)))
            else:
                v, sw = split(dot(bufs[(b - 1) % 2][i], w[n - 1]))
                dst[i, :, :wd] = rot(v, sw, 2 * n, i).astype(BF16).reshape(rows, wd)
            dst[i ^ 2**b, :, wd:] = rot(v, sw, 2 * n + 1, i).astype(BF16).reshape(rows, wd)

    for blocks in groups_of(S, MID_GROUPS):
        state = [split(dot(bufs[(src_bits - 1) % 2][i], w[K - 1])) for i in blocks]
        state = [rot(v, sw, I_MID, i).astype(BF16).reshape(rows, wd) for i, (v, sw) in zip(blocks, state)]
        state = [split(dot(x, wm[...])) for x in state]
        for b in range(tgt_bits):
            if b < tgt_bits - 1:
                state = [step(v, sw, K + b, i, 2**b) for i, (v, sw) in zip(blocks, state)]
            else:
                state = [last_step(v, sw, K + b, i, 2**b) for i, (v, sw) in zip(blocks, state)]
        for i, v in zip(blocks, state):
            send2[:, i] = v.astype(BF16)
    for k in range(AHEAD):
        c2_copy(k).start()
    for n in range(M, N):
        fill(w.at[n], 0, lint[n, 0])
        fill(w.at[n], 2 * half, lint[n, 1])
    fill(wf, 0, mats[2])
    for n in range(M, N):
        put_level(n, lp(n - 1, 2), lpair(n), 2 ** (n - M))
    put(I_FIN, lp(N - 1, 2) + dup(phases[2]))
    c, s = cos_sin(points[1])
    tc[I_TGT, 0 : R // 2] = c
    ts[I_TGT, 0 : R // 2] = s
    for k in range(AHEAD, T - 1):
        c2_copy(k).start()
    recv2[t_me] = send2[t_me]

    low3 = lane_low((rhs, wd), half)

    c2_all.wait_recv()
    for blocks in groups_of(S, FIN_GROUPS):
        state = []
        for i in blocks:
            v = recv2[:, i].reshape(rows, wd)
            state.append(tuple(x.astype(F32).reshape(T, rhs, wd) for x in (v, pltpu.roll(v, half, 1))))
        for n in range(M, N):
            state = [step(v, sw, n, i, 2 ** (n - M)) for i, (v, sw) in zip(blocks, state)]
        state = [rot(v, sw, I_FIN, i).astype(BF16).reshape(rows, wd) for i, (v, sw) in zip(blocks, state)]
        state = [split(dot(x, wf[...])) for x in state]
        for i, (v, sw) in zip(blocks, state):
            for p in range(T // 2):
                row = pl.ds(i * (T // 2) + p, 8, stride=0)
                c = jnp.concatenate([tc[I_TGT, row, :]] * (rhs // 8), 0)
                s = jnp.concatenate([ts[I_TGT, row, :]] * (rhs // 8), 0)
                re = jnp.where(low3, v[2 * p], sw[2 * p + 1])
                im = jnp.where(low3, sw[2 * p], v[2 * p + 1])
                col = pl.ds(i * T * half + p * wd, wd)
                out[0, :, col] = re * c - im * s
                out[1, :, col] = re * s + im * c
    ps_all.wait_send()
    pt_all.wait_send()
    c1_all.wait_send()
    c2_all.wait_send()


def shards(
    source_values, source_phase, leaf_interp, level_interp, level_phase,
    middle_interp, middle_phase, final_phase, final_interp, target_phase,
):
    S = lax.axis_size("src")
    T = lax.axis_size("tgt")
    R = level_phase.shape[2]
    assert R == S * T
    rhs = source_values.shape[0]
    half = leaf_interp.shape[1]
    wd = 2 * half
    N = level_phase.shape[0]
    src_bits = S.bit_length() - 1
    tgt_bits = T.bit_length() - 1
    assert N == LOCAL_SRC + src_bits + tgt_bits + LOCAL_TGT
    Q1 = src_bits + (src_bits + 1) // 2
    Q = 1 + tgt_bits + tgt_bits // 2
    ntab = 2 * N + 5
    vm = pltpu.VMEM
    dma = pltpu.SemaphoreType.DMA
    args = (
        source_values, source_phase.reshape(-1, wd), leaf_interp, level_interp, level_phase,
        middle_interp, middle_phase, final_phase, final_interp, target_phase.reshape(-1, wd),
    )
    return pl.pallas_call(
        functools.partial(kernel, S, T, N, src_bits, tgt_bits),
        out_shape=pltpu.VMEM((2,) + source_values.shape, F32),
        in_specs=[pl.BlockSpec(memory_space=pltpu.HBM)] * 10,
        out_specs=pl.BlockSpec(memory_space=pltpu.VMEM),
        scratch_shapes=[vm(args[i].shape, args[i].dtype) for i in (0, 3, 4)] + [
            vm((2,) + args[1].shape, F32), vm((3, half, half), BF16), vm((3, R, half), F32), dma((7,)),
            vm((N, 2 * wd, 2 * wd), BF16), vm((wd, 2 * wd), BF16),
            vm((wd, 2 * wd), BF16), vm((wd, 2 * wd), BF16),
            vm((ntab, R, wd), F32), vm((ntab, R, wd), F32),
            vm((S, Q1 * T, wd), SENT), vm((S, Q1 * T, wd), SENT), vm((Q * R, wd), F32),
            vm((T, Q * S, wd), SENT), vm((T, Q * S, wd), SENT), vm((T, Q * S, wd), F32),
            vm((S, T * rhs, wd), BF16),
            vm((S, T * rhs, 2 * wd), BF16), vm((S, T * rhs, 2 * wd), BF16),
            vm((T, S, rhs, wd), BF16), vm((T, S, rhs, wd), BF16),
            dma(()), dma(()), dma(()), dma(()),
        ],
        compiler_params=pltpu.CompilerParams(
            collective_id=0, has_side_effects=True, vmem_limit_bytes=VLIM
        ),
    )(*[pltpu.with_memory_space_constraint(a, pltpu.HBM) for a in args])


def solution(mesh):
    return jax.shard_map(
        shards,
        mesh=mesh,
        in_specs=(
            P(None, ("src", "tgt")),
            P(("src", "tgt")),
            P(),
            P(),
            P(None, None, ("src", "tgt"), None),
            P(),
            P(None, ("src", "tgt"), None),
            P(("src", "tgt"), None),
            P(),
            P(("src", "tgt")),
        ),
        out_specs=P(None, None, ("src", "tgt")),
        check_vma=False,
    )
```
